32 devices in a mesh: group: 2 (over y), tm: 16 (over z, x, core).
Axes of the slice: x: 2, y: 2, z: 4, core: 2. Of those that a mesh axis runs over, the one named last changes fastest.
Arguments:
- features: bfloat16 [64, 192, 8, 256], P(('group', 'tm')), parts along dimension 0, may hold values from -6 to 6
- video_frames: int32 [16], P('group'), parts along dimension 0, may hold values from 1 to 16, 32 in all
- gain_first: float32 [192], replicated, may hold values from 0.1 to 1.9
- conv_first: bfloat16 [3, 3, 3, 192, 192], replicated, may hold values from -0.078125 to 0.078125
- gain_second: float32 [192], replicated, may hold values from 0.1 to 1.9
- conv_second: bfloat16 [3, 3, 3, 192, 192], replicated, may hold values from -0.078125 to 0.078125
Outputs:
- block_out: bfloat16 [64, 192, 8, 256], P(('group', 'tm')), parts along dimension 0
The draws below stay inside these ranges and needn't reach their ends.
There are 2 independent parts, one for each index of `group`. The reference program is written for one: setup_inputs(seed, part) draws one part's arguments, and reference() takes and returns one part's arrays. A program takes and returns all parts, laid end to end along the dimension named above; an argument that names none is the same for every part. Nothing has to cross between parts.
Inputs may be any that keep to these rules, and one draw needn't show every extreme that they name: `video_frames`: each video's frame count; they sum to 32 and the largest is exactly 16.
All inputs are finite; a program needn't handle non-finite values.
Results may differ from the reference program's by a relative error of at most 0.0039.
Values may be sent and summed in bfloat16 or wider, within the bound.
No kernel may reach another device: no remote copies, remote signals or barrier semaphores. Data moves between devices by JAX's collectives and lax.ppermute only.
A program may use at most 128 MiB of HBM per device.

```python
import math
import jax
import jax.numpy as jnp
import numpy as np
from jax import lax

C = 192
ROWS = 8
COLS = 256
FRAMES = 32
VIDEOS = 8
MOST = 16


def block_levels(rng, dims, cuts, least, top_value):
    def one(axis_at, parts):
        heights = jax.random.uniform(jax.random.fold_in(jax.random.fold_in(rng, 6), axis_at), (parts,), jnp.float32, least / len(cuts), top_value / len(cuts))
        return jnp.repeat(jnp.exp(heights), dims[axis_at] // parts).reshape((-1,) + (1,) * (len(dims) - axis_at - 1))

    loudness = one(*cuts[0])
    for cut in cuts[1:]:
        loudness = loudness * one(*cut)
    return loudness


def profile(count, total, reach, slope):
    weights = [(1 << 20) // math.isqrt(rank ** slope) + 1 for rank in range(2, count + 1)]
    spare, counts = total - reach - (count - 1), [1] * (count - 1)
    while spare > 0:
        movable = [i for i in range(count - 1) if counts[i] < reach]
        whole, left = sum([weights[i] for i in movable]), spare
        for i in movable:
            extra = min(reach - counts[i], max(1, left * weights[i] // whole), spare)
            counts[i] = counts[i] + extra
            spare = spare - extra
    return np.array([reach] + counts)


def uneven_parts(key, number_of, total, most, slope):
    if number_of == 2:
        one = jax.random.randint(key, (), max(1, total - most), min(most, total - 1) + 1)
        return jnp.stack([one, total - one])
    tallies = jnp.asarray(profile(number_of, total, most, slope), jnp.int32)
    couples = (number_of - 1) // 2
    giver, taker = tallies[1:1 + 2 * couples:2], tallies[2:2 + 2 * couples:2]
    slack = jnp.minimum(giver - 1, most - taker)
    moved = jax.random.randint(jax.random.fold_in(key, 1), (couples,), 0, 1 << 20) % (slack + 1)
    tallies = tallies.at[1:1 + 2 * couples:2].set(giver - moved).at[2:2 + 2 * couples:2].set(taker + moved)
    return tallies[jax.random.permutation(jax.random.fold_in(key, 2), number_of)]


def centred(stream_key, extent, deviation, bound, split=(), kind=jnp.bfloat16):
    values = deviation * jax.random.normal(stream_key, extent, jnp.float32)
    if split:
        values = values * block_levels(stream_key, extent, split, -0.22, 0.18)
    return jnp.clip(values, -bound, bound).astype(kind)


def setup_inputs(seed: int = 0, part: int = 0) -> dict:
    keys = jax.random.split(jax.random.key(seed), 7)
    own_keys = jax.random.split(jax.random.fold_in(keys[6], part), 7)
    return {
        "features": centred(own_keys[0], (FRAMES, C, ROWS, COLS), 1.0, 6.0, ((0, 16),)),
        "video_frames": uneven_parts(own_keys[1], VIDEOS, FRAMES, MOST, 2).astype(jnp.int32),
        "gain_first": jnp.clip(1.0 + 0.18 * jax.random.normal(keys[2], (C,), jnp.float32), 0.1, 1.9),
        "conv_first": centred(keys[3], (3, 3, 3, C, C), (27 * C) ** -0.5, 0.078125),
        "gain_second": jnp.clip(1.0 + 0.18 * jax.random.normal(keys[4], (C,), jnp.float32), 0.1, 1.9),
        "conv_second": centred(keys[5], (3, 3, 3, C, C), (27 * C) ** -0.5, 0.078125),
    }


def video_start(video_frames, positions):
    video_ends = jnp.cumsum(video_frames).astype(jnp.int32)
    video_begins = (video_ends - video_frames).astype(jnp.int32)
    inside = video_begins[None, :] <= positions[:, None]
    return lax.optimization_barrier(jnp.max(jnp.where(inside, video_begins[None, :], 0), axis=1)).astype(jnp.int32)

def build_masks(video_frames, positions):
    starts = video_start(video_frames, positions)
    columns = [(positions - lag_tap >= starts).astype(jnp.float32) for lag_tap in range(3)]
    return jnp.stack(columns, axis=1)

def normalize(values, gain):
    mean_square = lax.optimization_barrier(jnp.mean(values * values, axis=1, keepdims=True))
    return values * lax.rsqrt(mean_square + 1e-06) * gain.astype(jnp.float32)[None, :, None, None]

def activate(values, gain):
    return jax.nn.silu(normalize(values, gain)).astype(jnp.bfloat16)

def causal_conv(padded, weights, masks):
    out_frames = padded.shape[0] - 2
    summed = None
    for lag_tap in range(3):
        frames = lax.slice_in_dim(padded, 2 - lag_tap, 2 - lag_tap + out_frames, axis=0)
        tapped = lax.conv_general_dilated(frames, weights[lag_tap], (1, 1), ((1, 1), (1, 1)), dimension_numbers=('NCHW', 'HWIO', 'NCHW'), preferred_element_type=jnp.float32)
        tapped = masks[:, lag_tap][:, None, None, None] * tapped
        summed = tapped if summed is None else summed + tapped
    return summed

def reference(features, video_frames, gain_first, conv_first, gain_second, conv_second):
    positions = jnp.arange(features.shape[0], dtype=jnp.int32)
    masks = build_masks(video_frames, positions)
    first_act = activate(features.astype(jnp.float32), gain_first)
    zero_pad = jnp.zeros((2,) + first_act.shape[1:], jnp.bfloat16)
    first_out = causal_conv(jnp.concatenate([zero_pad, first_act], axis=0), conv_first, masks)
    second_act = activate(first_out, gain_second)
    second_out = causal_conv(jnp.concatenate([zero_pad, second_act], axis=0), conv_second, masks)
    return (features.astype(jnp.float32) + second_out).astype(jnp.bfloat16)
```

```python
import jax
import jax.numpy as jnp
from jax import lax
from jax.experimental import pallas as pl
from jax.experimental.pallas import tpu as pltpu
from jax.sharding import PartitionSpec as P

C = 192
ROWS = 8
COLS = 256
HALF = 128
SLAB = 3 * C
DEPTH = 9 * C
EPS = 1e-06
VMEM_LIMIT = 48 * 1024 * 1024
F32 = jnp.float32
BF16 = jnp.bfloat16


def shifted(value, axis):
    count = lax.axis_size(axis)
    return lax.ppermute(value, axis, [(i, i + 1) for i in range(count - 1)])


def tap_masks(frames_ref, first):
    def step(v, carry):
        begin, start0, start1 = carry
        start0 = jnp.where(begin <= first, begin, start0)
        start1 = jnp.where(begin <= first + 1, begin, start1)
        return begin + frames_ref[v], start0, start1

    zero = jnp.int32(0)
    _, start0, start1 = lax.fori_loop(0, frames_ref.shape[0], step, (zero, zero, zero))
    return tuple(
        jnp.where(test, 1.0, 0.0).astype(F32)
        for test in (
            first - 1 >= start0,
            first - 2 >= start0,
            first >= start1,
            first - 1 >= start1,
        )
    )


def first_frame():
    return 2 * lax.axis_index("tm")


def transpose_weights(w_ref, wt_ref):
    for k in range(3):
        wt_ref[k * C : (k + 1) * C, :] = w_ref[k * DEPTH : (k + 1) * DEPTH, :].T


def put_row(x_ref, row, values):
    base = (row + 1) * SLAB
    cols = lax.broadcasted_iota(jnp.int32, (C, COLS), 1)
    left = jnp.where(cols == 0, 0.0, pltpu.roll(values, 1, 1))
    right = jnp.where(cols == COLS - 1, 0.0, pltpu.roll(values, COLS - 1, 1))
    x_ref[base : base + C, :] = left.astype(BF16)
    x_ref[base + C : base + 2 * C, :] = values.astype(BF16)
    x_ref[base + 2 * C : base + 3 * C, :] = right.astype(BF16)


def clear_edges(x_ref):
    zeros = jnp.zeros((SLAB, COLS), BF16)
    x_ref[0:SLAB, :] = zeros
    x_ref[(ROWS + 1) * SLAB : (ROWS + 2) * SLAB, :] = zeros


def activate_features(f_ref, gain_ref, t_ref, x_ref):
    def squares(b, total):
        v = f_ref[0, pl.ds(b * 16, 16)].astype(F32)
        return total + jnp.sum(v * v, axis=0)

    total = lax.fori_loop(0, C // 16, squares, jnp.zeros((ROWS, COLS), F32))
    inverse = lax.rsqrt(total * (1.0 / C) + EPS)

    def act(b, _):
        for j in range(8):
            c = b * 8 + j
            u = f_ref[0, c].astype(F32) * inverse * gain_ref[c]
            u = u * jax.nn.sigmoid(u)
            at = pl.multiple_of(c * ROWS, ROWS)
            t_ref[0, pl.ds(at, ROWS), :] = u[:, :HALF]
            t_ref[1, pl.ds(at, ROWS), :] = u[:, HALF:]
        return 0

    lax.fori_loop(0, C // 8, act, 0)
    clear_edges(x_ref)
    for row in range(ROWS):
        put_row(
            x_ref,
            row,
            jnp.concatenate(
                [t_ref[h, pl.ds(row, C, stride=ROWS), :] for h in range(2)], axis=1
            ),
        )


def slab_of(s_ref, x_ref):
    clear_edges(x_ref)
    for row in range(ROWS):
        put_row(x_ref, row, s_ref[row].astype(F32))


def product(wt_ref, lo, hi, x_ref, row):
    return jnp.dot(
        wt_ref[lo * C : hi * C, :],
        x_ref[row * SLAB : row * SLAB + DEPTH, :],
        preferred_element_type=F32,
    )


def spread_gain(gain_ref, g_ref):
    def step(b, _):
        for j in range(8):
            c = b * 8 + j
            g_ref[pl.ds(c, 1), :] = jnp.full((1, COLS), gain_ref[c], F32)
        return 0

    lax.fori_loop(0, C // 8, step, 0)


def second_activation(values, g_ref):
    mean_square = jnp.sum(values * values, axis=0, keepdims=True) * (1.0 / C)
    u = values * lax.rsqrt(mean_square + EPS) * g_ref[...]
    return (u * jax.nn.sigmoid(u)).astype(BF16)


def to_output(t_ref, f_ref, o_ref):
    def step(b, _):
        for j in range(8):
            c = b * 8 + j
            at = pl.multiple_of(c * ROWS, ROWS)
            v = jnp.concatenate(
                [t_ref[h, pl.ds(at, ROWS), :] for h in range(2)], axis=1
            )
            o_ref[0, c] = (f_ref[0, c].astype(F32) + v).astype(BF16)
        return 0

    lax.fori_loop(0, C // 8, step, 0)


def put_transposed(t_ref, row, values):
    t_ref[0, pl.ds(row, C, stride=ROWS), :] = values[:, :HALF]
    t_ref[1, pl.ds(row, C, stride=ROWS), :] = values[:, HALF:]


def local_first(f0_ref, f1_ref, w_ref, gain_ref, frames_ref, o_ref, wt_ref, t_ref, x_ref):
    _, _, v11, _ = tap_masks(frames_ref, first_frame())
    transpose_weights(w_ref, wt_ref)
    activate_features(f0_ref, gain_ref, t_ref, x_ref)
    for row in range(ROWS):
        d = product(wt_ref, 0, 2, x_ref, row)
        o_ref[0, row] = d[:C]
        o_ref[1, row] = v11 * d[C:]
    activate_features(f1_ref, gain_ref, t_ref, x_ref)
    for row in range(ROWS):
        o_ref[1, row] += product(wt_ref, 0, 1, x_ref, row)


def halo_first(
    h_ref, o_ref, wt_ref, gain_ref, gain2_ref, frames_ref, p_ref, s_ref, t_ref, x_ref, g_ref
):
    v01, _, _, v12 = tap_masks(frames_ref, first_frame())
    spread_gain(gain2_ref, g_ref)
    activate_features(h_ref, gain_ref, t_ref, x_ref)
    for row in range(ROWS):
        d = product(wt_ref, 1, 3, x_ref, row)
        p_ref[row] = o_ref[0, row] + v01 * d[:C]
        s_ref[row] = second_activation(o_ref[1, row] + v12 * d[C:], g_ref)


def halo_second(
    h_ref, p_ref, wt_ref, gain_ref, gain2_ref, frames_ref, s_ref, t_ref, x_ref, g_ref
):
    _, v02, _, _ = tap_masks(frames_ref, first_frame())
    spread_gain(gain2_ref, g_ref)
    activate_features(h_ref, gain_ref, t_ref, x_ref)
    for row in range(ROWS):
        d = product(wt_ref, 2, 3, x_ref, row)
        s_ref[row] = second_activation(p_ref[row] + v02 * d, g_ref)


def local_second(s0_ref, s1_ref, w_ref, frames_ref, o_ref, wt_ref, x_ref):
    _, _, v11, _ = tap_masks(frames_ref, first_frame())
    transpose_weights(w_ref, wt_ref)
    slab_of(s0_ref, x_ref)
    for row in range(ROWS):
        d = product(wt_ref, 0, 2, x_ref, row)
        o_ref[0, row] = d[:C]
        o_ref[1, row] = v11 * d[C:]
    slab_of(s1_ref, x_ref)
    for row in range(ROWS):
        o_ref[1, row] += product(wt_ref, 0, 1, x_ref, row)


def last_frame(h_ref, o_ref, wt_ref, f_ref, frames_ref, p_ref, out_ref, t_ref, x_ref):
    v01, _, _, v12 = tap_masks(frames_ref, first_frame())
    slab_of(h_ref, x_ref)
    for row in range(ROWS):
        d = product(wt_ref, 1, 3, x_ref, row)
        p_ref[row] = o_ref[0, row] + v01 * d[:C]
        put_transposed(t_ref, row, o_ref[1, row] + v12 * d[C:])
    to_output(t_ref, f_ref, out_ref)


def other_frame(h_ref, p_ref, wt_ref, f_ref, frames_ref, _, out_ref, t_ref, x_ref):
    _, v02, _, _ = tap_masks(frames_ref, first_frame())
    slab_of(h_ref, x_ref)
    for row in range(ROWS):
        d = product(wt_ref, 2, 3, x_ref, row)
        put_transposed(t_ref, row, p_ref[row] + v02 * d)
    to_output(t_ref, f_ref, out_ref)


VM = pl.BlockSpec(memory_space=pltpu.VMEM)
SM = pl.BlockSpec(memory_space=pltpu.SMEM)
ANY = pl.BlockSpec(memory_space=pl.ANY)
NATURAL = pltpu.VMEM((2, C * ROWS, HALF), F32)
SLABS = pltpu.VMEM(((ROWS + 2) * SLAB, COLS), BF16)
GAINS = pltpu.VMEM((C, COLS), F32)
PAIR = jax.ShapeDtypeStruct((2, ROWS, C, COLS), F32)
ONE = jax.ShapeDtypeStruct((ROWS, C, COLS), F32)
ACT = jax.ShapeDtypeStruct((ROWS, C, COLS), BF16)
TURNED = jax.ShapeDtypeStruct((3 * C, DEPTH), BF16)


def frame(i):
    return pl.BlockSpec((1, C, ROWS, COLS), lambda _: (i, 0, 0, 0))


def call(kernel, in_specs, out_specs, out_shape, scratch, name, aliases=None):
    return pl.pallas_call(
        kernel,
        grid=(1,),
        in_specs=in_specs,
        out_specs=out_specs,
        out_shape=out_shape,
        scratch_shapes=scratch,
        input_output_aliases=aliases or {},
        compiler_params=pltpu.CompilerParams(vmem_limit_bytes=VMEM_LIMIT),
        name=name,
    )


def per_device(features, video_frames, gain_first, conv_first, gain_second, conv_second):
    w1 = conv_first.reshape(3 * DEPTH, C)
    w2 = conv_second.reshape(3 * DEPTH, C)
    whole = jax.ShapeDtypeStruct(features.shape, BF16)
    before = shifted(features[1:], "tm")
    earlier = shifted(features[:1], "tm")

    sums, wt1 = call(
        local_first, [frame(0), frame(1), VM, SM, SM], [VM, VM], [PAIR, TURNED],
        [NATURAL, SLABS], "local_first",
    )(features, features, w1, gain_first, video_frames)
    part, s1 = call(
        halo_first, [VM, VM, VM, SM, SM, SM], [VM, VM], [ONE, ACT],
        [NATURAL, SLABS, GAINS], "halo_first",
    )(before, sums, wt1, gain_first, gain_second, video_frames)
    s_before = shifted(s1, "tm")
    s0 = call(
        halo_second, [VM, VM, VM, SM, SM, SM], VM, ACT,
        [NATURAL, SLABS, GAINS], "halo_second",
    )(earlier, part, wt1, gain_first, gain_second, video_frames)
    s_earlier = shifted(s0, "tm")
    sums2, wt2 = call(
        local_second, [VM, VM, VM, SM], [VM, VM], [PAIR, TURNED],
        [SLABS], "local_second",
    )(s0, s1, w2, video_frames)
    part2, out = call(
        last_frame, [VM, VM, VM, frame(1), SM], [VM, frame(1)], [ONE, whole],
        [NATURAL, SLABS], "last_frame",
    )(s_before, sums2, wt2, features, video_frames)
    return call(
        other_frame, [VM, VM, VM, frame(0), SM, ANY], frame(0), whole,
        [NATURAL, SLABS], "other_frame", {5: 0},
    )(s_earlier, part2, wt2, features, video_frames, out)


def solution(mesh):
    in_specs = (P(("group", "tm"), None, None, None), P("group"), P(), P(), P(), P())
    out_specs = P(("group", "tm"), None, None, None)
    return jax.shard_map(
        per_device, mesh=mesh, in_specs=in_specs, out_specs=out_specs, check_vma=False
    )
```

```python
import jax
import jax.numpy as jnp
from jax import lax
from jax.experimental import pallas as pl
from jax.experimental.pallas import tpu as pltpu
from jax.sharding import PartitionSpec as P

C = 192
ROWS = 8
COLS = 256
HALF = 128
TAPS = 3
SLAB = 3 * C
DEPTH = 9 * C
PIECE = 384
PARTS = 4
EPS = 1e-06
VMEM_LIMIT = 16 * 1024 * 1024
F32 = jnp.float32
BF16 = jnp.bfloat16


def shifted(value, axis):
    count = lax.axis_size(axis)
    return lax.ppermute(value, axis, [(i, i + 1) for i in range(count - 1)])


def tap_masks(frames_ref):
    first = 2 * lax.axis_index("tm")

    def step(v, carry):
        begin, start0, start1 = carry
        start0 = jnp.where(begin <= first, begin, start0)
        start1 = jnp.where(begin <= first + 1, begin, start1)
        return begin + frames_ref[v], start0, start1

    zero = jnp.int32(0)
    _, start0, start1 = lax.fori_loop(0, frames_ref.shape[0], step, (zero, zero, zero))
    return tuple(
        jnp.where(test, 1.0, 0.0).astype(F32)
        for test in (
            first - 1 >= start0,
            first - 2 >= start0,
            first >= start1,
            first - 1 >= start1,
        )
    )


def turn_pieces(w_ref, wt_ref, taps):
    def turn(k, lo, hi):
        wt_ref[k * C : (k + 1) * C, lo:hi] = w_ref[k * DEPTH + lo : k * DEPTH + hi, :].T

    return [
        (lambda k=k, lo=lo: turn(k, lo, min(lo + PIECE, DEPTH)))
        for k in taps
        for lo in range(0, DEPTH, PIECE)
    ]


def put_row(x_ref, row, values):
    base = (row + 1) * SLAB
    cols = lax.broadcasted_iota(jnp.int32, (C, COLS), 1)
    left = jnp.where(cols == 0, 0.0, pltpu.roll(values, 1, 1))
    right = jnp.where(cols == COLS - 1, 0.0, pltpu.roll(values, COLS - 1, 1))
    x_ref[base : base + C, :] = left.astype(BF16)
    x_ref[base + C : base + 2 * C, :] = values.astype(BF16)
    x_ref[base + 2 * C : base + 3 * C, :] = right.astype(BF16)


def clear_edges(x_ref):
    zeros = jnp.zeros((SLAB, COLS), BF16)
    x_ref[0:SLAB, :] = zeros
    x_ref[(ROWS + 1) * SLAB : (ROWS + 2) * SLAB, :] = zeros


def put(x_ref, a_ref, row):
    if row < ROWS:
        put_row(x_ref, row, a_ref[row].astype(F32))


def product(wt_ref, lo, hi, x_ref, row):
    return jnp.dot(
        wt_ref[lo * C : hi * C, :],
        x_ref[row * SLAB : row * SLAB + DEPTH, :],
        preferred_element_type=F32,
    )


def activation(index):
    def kernel(f_ref, gain_ref, a_ref, t_ref):
        def squares(b, total):
            v = f_ref[index, pl.ds(b * 16, 16)].astype(F32)
            return total + jnp.sum(v * v, axis=0)

        total = lax.fori_loop(0, C // 16, squares, jnp.zeros((ROWS, COLS), F32))
        inverse = lax.rsqrt(total * (1.0 / C) + EPS)

        def act(b, _):
            for j in range(16):
                c = b * 16 + j
                u = f_ref[index, c].astype(F32) * inverse * gain_ref[c]
                u = u * jax.nn.sigmoid(u)
                at = pl.multiple_of(c * ROWS, ROWS)
                t_ref[0, pl.ds(at, ROWS), :] = u[:, :HALF]
                t_ref[1, pl.ds(at, ROWS), :] = u[:, HALF:]
            return 0

        lax.fori_loop(0, C // 16, act, 0)
        for row in range(ROWS):
            for h in range(2):
                a_ref[row, :, h * HALF : (h + 1) * HALF] = t_ref[
                    h, pl.ds(row, C, stride=ROWS), :
                ].astype(BF16)

    return kernel


def spread_gain(gain_ref, g_ref):
    def step(b, _):
        for j in range(8):
            c = b * 8 + j
            g_ref[pl.ds(c, 1), :] = jnp.full((1, COLS), gain_ref[c], F32)
        return 0

    lax.fori_loop(0, C // 8, step, 0)


def second_activation(values, g_ref):
    mean_square = jnp.sum(values * values, axis=0, keepdims=True) * (1.0 / C)
    u = values * lax.rsqrt(mean_square + EPS) * g_ref[...]
    return (u * jax.nn.sigmoid(u)).astype(BF16)


def put_transposed(t_ref, row, values):
    t_ref[0, pl.ds(row, C, stride=ROWS), :] = values[:, :HALF]
    t_ref[1, pl.ds(row, C, stride=ROWS), :] = values[:, HALF:]


def write_frame(index, t_ref, f_ref, buf_ref, out_ref, sems):
    step = C // PARTS

    def piece(p):
        span = pl.ds(p * step, step)
        return pltpu.make_async_copy(buf_ref.at[span], out_ref.at[index, span], sems.at[p])

    for p in range(PARTS):

        def add(b, _):
            for j in range(16):
                c = p * step + b * 16 + j
                at = pl.multiple_of(c * ROWS, ROWS)
                v = jnp.concatenate([t_ref[h, pl.ds(at, ROWS), :] for h in range(2)], axis=1)
                buf_ref[c] = (f_ref[index, c].astype(F32) + v).astype(BF16)
            return 0

        lax.fori_loop(0, step // 16, add, 0)
        piece(p).start()
    for p in range(PARTS):
        piece(p).wait()


def both_frames(a0_ref, a1_ref, v11, wt_ref, o0_ref, o1_ref, x0_ref, x1_ref, extra):
    clear_edges(x0_ref)
    clear_edges(x1_ref)
    put(x0_ref, a0_ref, 0)
    put(x0_ref, a0_ref, 1)
    extra = list(extra)
    share = -(-len(extra) // ROWS)
    for row in range(ROWS):
        d = product(wt_ref, 0, 2, x0_ref, row)
        put(x0_ref, a0_ref, row + 2)
        put(x1_ref, a1_ref, row)
        for step in extra[row * share : (row + 1) * share]:
            step()
        o0_ref[row] = d[:C]
        o1_ref[row] = v11 * d[C:]
    for row in range(ROWS):
        o1_ref[row] += product(wt_ref, 0, 1, x1_ref, row)


def local_first(
    a0_ref, a1_ref, w1_ref, w2_ref, frames_ref, o0_ref, o1_ref, wt1_ref, wt2_ref, x0_ref, x1_ref
):
    _, _, v11, _ = tap_masks(frames_ref)
    for step in turn_pieces(w1_ref, wt1_ref, (0, 1)):
        step()
    later = turn_pieces(w1_ref, wt1_ref, (2,)) + turn_pieces(w2_ref, wt2_ref, (0, 1, 2))
    both_frames(a0_ref, a1_ref, v11, wt1_ref, o0_ref, o1_ref, x0_ref, x1_ref, later)


def local_second(a0_ref, a1_ref, wt_ref, frames_ref, o0_ref, o1_ref, x0_ref, x1_ref):
    _, _, v11, _ = tap_masks(frames_ref)
    both_frames(a0_ref, a1_ref, v11, wt_ref, o0_ref, o1_ref, x0_ref, x1_ref, ())


def halo_first(h_ref, o0_ref, o1_ref, wt_ref, gain_ref, frames_ref, p_ref, s_ref, x_ref, g_ref):
    v01, _, _, v12 = tap_masks(frames_ref)
    spread_gain(gain_ref, g_ref)
    clear_edges(x_ref)
    put(x_ref, h_ref, 0)
    put(x_ref, h_ref, 1)
    for row in range(ROWS):
        d = product(wt_ref, 1, 3, x_ref, row)
        put(x_ref, h_ref, row + 2)
        p_ref[row] = o0_ref[row] + v01 * d[:C]
        s_ref[row] = second_activation(o1_ref[row] + v12 * d[C:], g_ref)


def halo_second(h_ref, p_ref, wt_ref, gain_ref, frames_ref, s_ref, x_ref, g_ref):
    _, v02, _, _ = tap_masks(frames_ref)
    spread_gain(gain_ref, g_ref)
    clear_edges(x_ref)
    put(x_ref, h_ref, 0)
    put(x_ref, h_ref, 1)
    for row in range(ROWS):
        d = product(wt_ref, 2, 3, x_ref, row)
        put(x_ref, h_ref, row + 2)
        s_ref[row] = second_activation(p_ref[row] + v02 * d, g_ref)


def last_frame(
    h_ref, o0_ref, o1_ref, wt_ref, f_ref, frames_ref, p_ref, out_ref, t_ref, x_ref, buf_ref, sems
):
    v01, _, _, v12 = tap_masks(frames_ref)
    clear_edges(x_ref)
    put(x_ref, h_ref, 0)
    put(x_ref, h_ref, 1)
    for row in range(ROWS):
        d = product(wt_ref, 1, 3, x_ref, row)
        put(x_ref, h_ref, row + 2)
        p_ref[row] = o0_ref[row] + v01 * d[:C]
        put_transposed(t_ref, row, o1_ref[row] + v12 * d[C:])
    write_frame(1, t_ref, f_ref, buf_ref, out_ref, sems)


def other_frame(
    h_ref, p_ref, wt_ref, f_ref, frames_ref, _, out_ref, t_ref, x_ref, buf_ref, sems
):
    _, v02, _, _ = tap_masks(frames_ref)
    clear_edges(x_ref)
    put(x_ref, h_ref, 0)
    put(x_ref, h_ref, 1)
    for row in range(ROWS):
        d = product(wt_ref, 2, 3, x_ref, row)
        put(x_ref, h_ref, row + 2)
        put_transposed(t_ref, row, p_ref[row] + v02 * d)
    write_frame(0, t_ref, f_ref, buf_ref, out_ref, sems)


VM = pl.BlockSpec(memory_space=pltpu.VMEM)
SM = pl.BlockSpec(memory_space=pltpu.SMEM)
ANY = pl.BlockSpec(memory_space=pl.ANY)
NATURAL = pltpu.VMEM((2, C * ROWS, HALF), F32)
SLABS = pltpu.VMEM(((ROWS + 2) * SLAB, COLS), BF16)
GAINS = pltpu.VMEM((C, COLS), F32)
FRAME = pltpu.VMEM((C, ROWS, COLS), BF16)
SEMS = pltpu.SemaphoreType.DMA((PARTS,))
SUM = jax.ShapeDtypeStruct((ROWS, C, COLS), F32)
ACT = jax.ShapeDtypeStruct((ROWS, C, COLS), BF16)
TURNED = jax.ShapeDtypeStruct((TAPS * C, DEPTH), BF16)


def call(kernel, in_specs, out_specs, out_shape, scratch, name, aliases=None):
    return pl.pallas_call(
        kernel,
        in_specs=in_specs,
        out_specs=out_specs,
        out_shape=out_shape,
        scratch_shapes=scratch,
        input_output_aliases=aliases or {},
        compiler_params=pltpu.CompilerParams(vmem_limit_bytes=VMEM_LIMIT),
        name=name,
    )


def per_device(features, video_frames, gain_first, conv_first, gain_second, conv_second):
    w1 = conv_first.reshape(TAPS * DEPTH, C)
    w2 = conv_second.reshape(TAPS * DEPTH, C)
    whole = jax.ShapeDtypeStruct(features.shape, BF16)

    a1, a0 = (
        call(activation(i), [VM, SM], VM, ACT, [NATURAL], f"activation_{i}")(features, gain_first)
        for i in (1, 0)
    )
    a_before = shifted(a1, "tm")
    a_earlier = shifted(a0, "tm")
    o0, o1, wt1, wt2 = call(
        local_first, [VM] * 4 + [SM], [VM] * 4, [SUM, SUM, TURNED, TURNED],
        [SLABS, SLABS], "local_first",
    )(a0, a1, w1, w2, video_frames)
    part, s1 = call(
        halo_first, [VM] * 4 + [SM, SM], [VM, VM], [SUM, ACT], [SLABS, GAINS], "halo_first",
    )(a_before, o0, o1, wt1, gain_second, video_frames)
    s_before = shifted(s1, "tm")
    s0 = call(
        halo_second, [VM] * 3 + [SM, SM], VM, ACT, [SLABS, GAINS], "halo_second",
    )(a_earlier, part, wt1, gain_second, video_frames)
    s_earlier = shifted(s0, "tm")
    q0, q1 = call(
        local_second, [VM] * 3 + [SM], [VM] * 2, [SUM, SUM], [SLABS, SLABS], "local_second",
    )(s0, s1, wt2, video_frames)
    part2, out = call(
        last_frame, [VM] * 5 + [SM], [VM, ANY], [SUM, whole],
        [NATURAL, SLABS, FRAME, SEMS], "last_frame",
    )(s_before, q0, q1, wt2, features, video_frames)
    return call(
        other_frame, [VM] * 4 + [SM, ANY], ANY, whole,
        [NATURAL, SLABS, FRAME, SEMS], "other_frame", {5: 0},
    )(s_earlier, part2, wt2, features, video_frames, out)


def solution(mesh):
    in_specs = (P(("group", "tm"), None, None, None), P("group"), P(), P(), P(), P())
    out_specs = P(("group", "tm"), None, None, None)
    return jax.shard_map(
        per_device, mesh=mesh, in_specs=in_specs, out_specs=out_specs, check_vma=False
    )
```

```python
import jax
import jax.numpy as jnp
from jax import lax
from jax.experimental import pallas as pl
from jax.experimental.pallas import tpu as pltpu
from jax.sharding import PartitionSpec as P

C = 192
ROWS = 8
COLS = 256
HALF = 128
TAPS = 3
SLAB = 3 * C
DEPTH = 9 * C
PIECE = 384
PARTS = 4
EPS = 1e-06
VMEM_LIMIT = 16 * 1024 * 1024
F32 = jnp.float32
BF16 = jnp.bfloat16


def shifted(value, axis):
    count = lax.axis_size(axis)
    return lax.ppermute(value, axis, [(i, i + 1) for i in range(count - 1)])


def tap_masks(frames_ref):
    first = 2 * lax.axis_index("tm")

    def step(v, carry):
        begin, start0, start1 = carry
        start0 = jnp.where(begin <= first, begin, start0)
        start1 = jnp.where(begin <= first + 1, begin, start1)
        return begin + frames_ref[v], start0, start1

    zero = jnp.int32(0)
    _, start0, start1 = lax.fori_loop(0, frames_ref.shape[0], step, (zero, zero, zero))
    return tuple(
        jnp.where(test, 1.0, 0.0).astype(F32)
        for test in (
            first - 1 >= start0,
            first - 2 >= start0,
            first >= start1,
            first - 1 >= start1,
        )
    )


def turn_pieces(w_ref, wt_ref, taps):
    def turn(k, lo, hi):
        wt_ref[k * C : (k + 1) * C, lo:hi] = w_ref[k * DEPTH + lo : k * DEPTH + hi, :].T

    return [
        (lambda k=k, lo=lo: turn(k, lo, min(lo + PIECE, DEPTH)))
        for k in taps
        for lo in range(0, DEPTH, PIECE)
    ]


def put_row(x_ref, row, values):
    base = (row + 1) * SLAB
    cols = lax.broadcasted_iota(jnp.int32, (C, COLS), 1)
    left = jnp.where(cols == 0, 0.0, pltpu.roll(values, 1, 1))
    right = jnp.where(cols == COLS - 1, 0.0, pltpu.roll(values, COLS - 1, 1))
    x_ref[base : base + C, :] = left.astype(BF16)
    x_ref[base + C : base + 2 * C, :] = values.astype(BF16)
    x_ref[base + 2 * C : base + 3 * C, :] = right.astype(BF16)


def clear_edges(x_ref):
    zeros = jnp.zeros((SLAB, COLS), BF16)
    x_ref[0:SLAB, :] = zeros
    x_ref[(ROWS + 1) * SLAB : (ROWS + 2) * SLAB, :] = zeros


def put(x_ref, a_ref, row):
    if row < ROWS:
        put_row(x_ref, row, a_ref[row].astype(F32))


def product(wt_ref, lo, hi, x_ref, row):
    return jnp.dot(
        wt_ref[lo * C : hi * C, :],
        x_ref[row * SLAB : row * SLAB + DEPTH, :],
        preferred_element_type=F32,
    )


def activation(index):
    def kernel(f_ref, gain_any, a_ref, raw_ref, gain_ref, t_ref, sems):
        copies = [
            pltpu.make_async_copy(
                f_ref.at[index, pl.ds(q * C // 2, C // 2), :, pl.ds(h * HALF, HALF)],
                raw_ref.at[h, pl.ds(q * C // 2, C // 2)],
                sems.at[2 * h + q],
            )
            for h in range(2)
            for q in range(2)
        ]
        gains = pltpu.make_async_copy(gain_any, gain_ref, sems.at[4])
        copies[0].start()
        copies[1].start()
        gains.start()
        copies[2].start()
        copies[3].start()
        for h in range(2):
            copies[2 * h].wait()
            copies[2 * h + 1].wait()

            def squares(b, total):
                v = raw_ref[h, pl.ds(b * 16, 16)].astype(F32)
                return total + jnp.sum(v * v, axis=0)

            total = lax.fori_loop(0, C // 16, squares, jnp.zeros((ROWS, HALF), F32))
            inverse = lax.rsqrt(total * (1.0 / C) + EPS)
            if h == 0:
                gains.wait()

            def act(b, _):
                for j in range(16):
                    c = b * 16 + j
                    u = raw_ref[h, c].astype(F32) * inverse * gain_ref[c]
                    t_ref[h, pl.ds(pl.multiple_of(c * ROWS, ROWS), ROWS), :] = u * jax.nn.sigmoid(u)
                return 0

            lax.fori_loop(0, C // 16, act, 0)
            for row in range(ROWS):
                a_ref[row, :, h * HALF : (h + 1) * HALF] = t_ref[
                    h, pl.ds(row, C, stride=ROWS), :
                ].astype(BF16)

    return kernel


def spread_gain(gain_ref, g_ref):
    def step(b, _):
        for j in range(8):
            c = b * 8 + j
            g_ref[pl.ds(c, 1), :] = jnp.full((1, COLS), gain_ref[c], F32)
        return 0

    lax.fori_loop(0, C // 8, step, 0)


def second_activation(values, g_ref):
    mean_square = jnp.sum(values * values, axis=0, keepdims=True) * (1.0 / C)
    u = values * lax.rsqrt(mean_square + EPS) * g_ref[...]
    return (u * jax.nn.sigmoid(u)).astype(BF16)


def put_transposed(t_ref, row, values):
    t_ref[0, pl.ds(row, C, stride=ROWS), :] = values[:, :HALF]
    t_ref[1, pl.ds(row, C, stride=ROWS), :] = values[:, HALF:]


def write_frame(index, t_ref, f_ref, buf_ref, out_ref, sems):
    step = C // PARTS

    def piece(p):
        span = pl.ds(p * step, step)
        return pltpu.make_async_copy(buf_ref.at[span], out_ref.at[index, span], sems.at[p])

    for p in range(PARTS):

        def add(b, _):
            for j in range(16):
                c = p * step + b * 16 + j
                at = pl.multiple_of(c * ROWS, ROWS)
                v = jnp.concatenate([t_ref[h, pl.ds(at, ROWS), :] for h in range(2)], axis=1)
                buf_ref[c] = (f_ref[index, c].astype(F32) + v).astype(BF16)
            return 0

        lax.fori_loop(0, step // 16, add, 0)
        piece(p).start()
    for p in range(PARTS):
        piece(p).wait()


def both_frames(a0_ref, a1_ref, v11, wt_ref, o0_ref, o1_ref, x0_ref, x1_ref, extra):
    clear_edges(x0_ref)
    clear_edges(x1_ref)
    put(x0_ref, a0_ref, 0)
    put(x0_ref, a0_ref, 1)
    for row in range(ROWS):
        d = product(wt_ref, 0, 2, x0_ref, row)
        put(x0_ref, a0_ref, row + 2)
        put(x1_ref, a1_ref, row)
        for step in extra.get(row, ()):
            step()
        o0_ref[row] = d[:C]
        o1_ref[row] = v11 * d[C:]
    for row in range(ROWS):
        d = product(wt_ref, 0, 1, x1_ref, row)
        for step in extra.get(ROWS + row, ()):
            step()
        o1_ref[row] += d


def local_first(
    a0_ref, a1_ref, w1_ref, w2_any, frames_ref,
    o0_ref, o1_ref, wt1_ref, wt2_ref, x0_ref, x1_ref, w2_ref, sems,
):
    third = TAPS * DEPTH // 3
    loads = [
        pltpu.make_async_copy(
            w2_any.at[pl.ds(k * third, third)], w2_ref.at[pl.ds(k * third, third)], sems.at[k]
        )
        for k in range(3)
    ]
    for load in loads:
        load.start()
    _, _, v11, _ = tap_masks(frames_ref)
    for step in turn_pieces(w1_ref, wt1_ref, (0, 1)):
        step()
    extra = {i: [step] for i, step in enumerate(turn_pieces(w1_ref, wt1_ref, (2,)))}
    later = turn_pieces(w2_ref, wt2_ref, (0, 1, 2))
    first = len(extra)
    for i, step in enumerate(later):
        extra.setdefault(first + i * (2 * ROWS - first) // len(later), []).append(step)
    for k in range(3):
        at = first + k * 5 * (2 * ROWS - first) // len(later)
        steps = extra[at]
        steps.insert(steps.index(later[5 * k]), loads[k].wait)
    both_frames(a0_ref, a1_ref, v11, wt1_ref, o0_ref, o1_ref, x0_ref, x1_ref, extra)


def local_second(a0_ref, a1_ref, wt_ref, frames_ref, o0_ref, o1_ref, x0_ref, x1_ref):
    _, _, v11, _ = tap_masks(frames_ref)
    both_frames(a0_ref, a1_ref, v11, wt_ref, o0_ref, o1_ref, x0_ref, x1_ref, {})


def halo_first(h_ref, o1_ref, wt_ref, gain_ref, frames_ref, s_ref, x_ref, g_ref):
    _, _, _, v12 = tap_masks(frames_ref)
    spread_gain(gain_ref, g_ref)
    clear_edges(x_ref)
    put(x_ref, h_ref, 0)
    put(x_ref, h_ref, 1)
    for row in range(ROWS):
        d = product(wt_ref, 2, 3, x_ref, row)
        put(x_ref, h_ref, row + 2)
        s_ref[row] = second_activation(o1_ref[row] + v12 * d, g_ref)


def halo_middle(o0_ref, x_ref, wt_ref, frames_ref, p_ref):
    v01, _, _, _ = tap_masks(frames_ref)
    for row in range(ROWS):
        p_ref[row] = o0_ref[row] + v01 * product(wt_ref, 1, 2, x_ref, row)


def halo_second(h_ref, p_ref, wt_ref, gain_ref, frames_ref, s_ref, x_ref, g_ref):
    _, v02, _, _ = tap_masks(frames_ref)
    spread_gain(gain_ref, g_ref)
    clear_edges(x_ref)
    put(x_ref, h_ref, 0)
    put(x_ref, h_ref, 1)
    for row in range(ROWS):
        d = product(wt_ref, 2, 3, x_ref, row)
        put(x_ref, h_ref, row + 2)
        s_ref[row] = second_activation(p_ref[row] + v02 * d, g_ref)


def last_frame(
    h_ref, o0_ref, o1_ref, wt_ref, f_ref, frames_ref, p_ref, out_ref, t_ref, x_ref, buf_ref, sems
):
    v01, _, _, v12 = tap_masks(frames_ref)
    clear_edges(x_ref)
    put(x_ref, h_ref, 0)
    put(x_ref, h_ref, 1)
    for row in range(ROWS):
        d = product(wt_ref, 1, 3, x_ref, row)
        put(x_ref, h_ref, row + 2)
        p_ref[row] = o0_ref[row] + v01 * d[:C]
        put_transposed(t_ref, row, o1_ref[row] + v12 * d[C:])
    write_frame(1, t_ref, f_ref, buf_ref, out_ref, sems)


def other_frame(
    h_ref, p_ref, wt_ref, f_ref, frames_ref, _, out_ref, t_ref, x_ref, buf_ref, sems
):
    _, v02, _, _ = tap_masks(frames_ref)
    clear_edges(x_ref)
    put(x_ref, h_ref, 0)
    put(x_ref, h_ref, 1)
    for row in range(ROWS):
        d = product(wt_ref, 2, 3, x_ref, row)
        put(x_ref, h_ref, row + 2)
        put_transposed(t_ref, row, p_ref[row] + v02 * d)
    write_frame(0, t_ref, f_ref, buf_ref, out_ref, sems)


VM = pl.BlockSpec(memory_space=pltpu.VMEM)
SM = pl.BlockSpec(memory_space=pltpu.SMEM)
ANY = pl.BlockSpec(memory_space=pl.ANY)
HBM = pl.BlockSpec(memory_space=pltpu.HBM)
NATURAL = pltpu.VMEM((2, C * ROWS, HALF), F32)
SLABS = pltpu.VMEM(((ROWS + 2) * SLAB, COLS), BF16)
GAINS = pltpu.VMEM((C, COLS), F32)
FRAME = pltpu.VMEM((C, ROWS, COLS), BF16)
SEMS = pltpu.SemaphoreType.DMA((PARTS,))
RAW = pltpu.VMEM((2, C, ROWS, HALF), BF16)
GAIN = pltpu.SMEM((C,), F32)
WEIGHTS = pltpu.VMEM((TAPS * DEPTH, C), BF16)
SLAB_ARRAY = jax.ShapeDtypeStruct(((ROWS + 2) * SLAB, COLS), BF16)
SUM = jax.ShapeDtypeStruct((ROWS, C, COLS), F32)
ACT = jax.ShapeDtypeStruct((ROWS, C, COLS), BF16)
TURNED = jax.ShapeDtypeStruct((TAPS * C, DEPTH), BF16)


def stay(value):
    return pltpu.with_memory_space_constraint(value, pltpu.HBM)


def call(kernel, in_specs, out_specs, out_shape, scratch, name, aliases=None):
    return pl.pallas_call(
        kernel,
        in_specs=in_specs,
        out_specs=out_specs,
        out_shape=out_shape,
        scratch_shapes=scratch,
        input_output_aliases=aliases or {},
        compiler_params=pltpu.CompilerParams(vmem_limit_bytes=VMEM_LIMIT),
        name=name,
    )


def per_device(features, video_frames, gain_first, conv_first, gain_second, conv_second):
    w1 = conv_first.reshape(TAPS * DEPTH, C)
    w2 = conv_second.reshape(TAPS * DEPTH, C)
    whole = jax.ShapeDtypeStruct(features.shape, BF16)

    a1, a0 = (
        call(
            activation(i), [HBM, HBM], VM, ACT, [RAW, GAIN, NATURAL, pltpu.SemaphoreType.DMA((5,))],
            f"activation_{i}",
        )(stay(features), stay(gain_first))
        for i in (1, 0)
    )
    a_before = shifted(a1, "tm")
    a_earlier = shifted(a0, "tm")
    o0, o1, wt1, wt2 = call(
        local_first, [VM] * 3 + [HBM, SM], [VM] * 4, [SUM, SUM, TURNED, TURNED],
        [SLABS, SLABS, WEIGHTS, pltpu.SemaphoreType.DMA((3,))], "local_first",
    )(a0, a1, w1, stay(w2), video_frames)
    s1, x = call(
        halo_first, [VM] * 3 + [SM, SM], [VM, VM], [ACT, SLAB_ARRAY], [GAINS], "halo_first",
    )(a_before, o1, wt1, gain_second, video_frames)
    s_before = shifted(s1, "tm")
    part = call(
        halo_middle, [VM] * 3 + [SM], VM, SUM, [], "halo_middle",
    )(o0, x, wt1, video_frames)
    s0 = call(
        halo_second, [VM] * 3 + [SM, SM], VM, ACT, [SLABS, GAINS], "halo_second",
    )(a_earlier, part, wt1, gain_second, video_frames)
    s_earlier = shifted(s0, "tm")
    q0, q1 = call(
        local_second, [VM] * 3 + [SM], [VM] * 2, [SUM, SUM], [SLABS, SLABS], "local_second",
    )(s0, s1, wt2, video_frames)
    part2, out = call(
        last_frame, [VM] * 5 + [SM], [VM, ANY], [SUM, whole],
        [NATURAL, SLABS, FRAME, SEMS], "last_frame",
    )(s_before, q0, q1, wt2, features, video_frames)
    return call(
        other_frame, [VM] * 4 + [SM, ANY], ANY, whole,
        [NATURAL, SLABS, FRAME, SEMS], "other_frame", {5: 0},
    )(s_earlier, part2, wt2, features, video_frames, out)


def solution(mesh):
    in_specs = (P(("group", "tm"), None, None, None), P("group"), P(), P(), P(), P())
    out_specs = P(("group", "tm"), None, None, None)
    return jax.shard_map(
        per_device, mesh=mesh, in_specs=in_specs, out_specs=out_specs, check_vma=False
    )
```

```python
import jax
import jax.numpy as jnp
from jax import lax
from jax.experimental import pallas as pl
from jax.experimental.pallas import tpu as pltpu
from jax.sharding import PartitionSpec as P

C = 192
ROWS = 8
COLS = 256
HALF = 128
TAPS = 3
SLAB = 3 * C
DEPTH = 9 * C
PIECE = 384
PARTS = 4
EPS = 1e-06
VMEM_LIMIT = 16 * 1024 * 1024
F32 = jnp.float32
BF16 = jnp.bfloat16


def shifted(value, axis):
    count = lax.axis_size(axis)
    return lax.ppermute(value, axis, [(i, i + 1) for i in range(count - 1)])


def tap_masks(frames_ref):
    first = 2 * lax.axis_index("tm")

    def step(v, carry):
        begin, start0, start1 = carry
        start0 = jnp.where(begin <= first, begin, start0)
        start1 = jnp.where(begin <= first + 1, begin, start1)
        return begin + frames_ref[v], start0, start1

    zero = jnp.int32(0)
    _, start0, start1 = lax.fori_loop(0, frames_ref.shape[0], step, (zero, zero, zero))
    return tuple(
        jnp.where(test, 1.0, 0.0).astype(F32)
        for test in (
            first - 1 >= start0,
            first - 2 >= start0,
            first >= start1,
            first - 1 >= start1,
        )
    )


def mask(m_ref, i):
    return m_ref[i : i + 1, :]


def turn_pieces(w_ref, wt_ref, taps):
    def turn(k, lo, hi):
        wt_ref[k * C : (k + 1) * C, lo:hi] = w_ref[k * DEPTH + lo : k * DEPTH + hi, :].T

    return [
        (lambda k=k, lo=lo: turn(k, lo, min(lo + PIECE, DEPTH)))
        for k in taps
        for lo in range(0, DEPTH, PIECE)
    ]


def put_row(x_ref, row, values):
    base = (row + 1) * SLAB
    cols = lax.broadcasted_iota(jnp.int32, (C, COLS), 1)
    left = jnp.where(cols == 0, 0.0, pltpu.roll(values, 1, 1))
    right = jnp.where(cols == COLS - 1, 0.0, pltpu.roll(values, COLS - 1, 1))
    x_ref[base : base + C, :] = left.astype(BF16)
    x_ref[base + C : base + 2 * C, :] = values.astype(BF16)
    x_ref[base + 2 * C : base + 3 * C, :] = right.astype(BF16)


def clear_edges(x_ref):
    zeros = jnp.zeros((SLAB, COLS), BF16)
    x_ref[0:SLAB, :] = zeros
    x_ref[(ROWS + 1) * SLAB : (ROWS + 2) * SLAB, :] = zeros


def put(x_ref, a_ref, row):
    if row < ROWS:
        put_row(x_ref, row, a_ref[row].astype(F32))


def product(wt_ref, lo, hi, x_ref, row):
    return jnp.dot(
        wt_ref[lo * C : hi * C, :],
        x_ref[row * SLAB : row * SLAB + DEPTH, :],
        preferred_element_type=F32,
    )


def inverse_rms(raw_ref, h):
    def squares(b, total):
        v = raw_ref[h, pl.ds(b * 16, 16)].astype(F32)
        return total + jnp.sum(v * v, axis=0)

    total = lax.fori_loop(0, C // 16, squares, jnp.zeros((ROWS, HALF), F32))
    return lax.rsqrt(total * (1.0 / C) + EPS)


def activate(raw_ref, h, c, inverse, gain_ref, t_ref):
    u = raw_ref[h, c].astype(F32) * inverse * gain_ref[c]
    at = c * ROWS if isinstance(c, int) else pl.multiple_of(c * ROWS, ROWS)
    t_ref[h, pl.ds(at, ROWS), :] = u * jax.nn.sigmoid(u)


def to_rows(t_ref, h, a_ref):
    for row in range(ROWS):
        a_ref[row, :, h * HALF : (h + 1) * HALF] = t_ref[
            h, pl.ds(row, C, stride=ROWS), :
        ].astype(BF16)


def frame_copies(f_ref, index, raw_ref, sems):
    return [
        [
            pltpu.make_async_copy(
                f_ref.at[index, pl.ds(q * C // 2, C // 2), :, pl.ds(h * HALF, HALF)],
                raw_ref.at[h, pl.ds(q * C // 2, C // 2)],
                sems.at[2 * h + q],
            )
            for q in range(2)
        ]
        for h in range(2)
    ]


def activate_last(f_ref, gain_any, a_ref, raw0_ref, raw1_ref, gain_ref, t_ref, sems, sems0):
    copies = frame_copies(f_ref, 1, raw1_ref, sems)
    others = frame_copies(f_ref, 0, raw0_ref, sems0)
    gains = pltpu.make_async_copy(gain_any, gain_ref, sems.at[4])
    for copy in copies[0] + [gains] + copies[1] + others[0] + others[1]:
        copy.start()
    for h in range(2):
        for copy in copies[h]:
            copy.wait()
        inverse = inverse_rms(raw1_ref, h)
        if h == 0:
            gains.wait()

        def act(b, _):
            for j in range(16):
                activate(raw1_ref, h, b * 16 + j, inverse, gain_ref, t_ref)
            return 0

        lax.fori_loop(0, C // 16, act, 0)
        to_rows(t_ref, h, a_ref)
    for copy in others[0] + others[1]:
        copy.wait()


def second_activation(values, g_ref):
    mean_square = jnp.sum(values * values, axis=0, keepdims=True) * (1.0 / C)
    u = values * lax.rsqrt(mean_square + EPS) * g_ref[...]
    return (u * jax.nn.sigmoid(u)).astype(BF16)


def put_transposed(t_ref, row, values):
    t_ref[0, pl.ds(row, C, stride=ROWS), :] = values[:, :HALF]
    t_ref[1, pl.ds(row, C, stride=ROWS), :] = values[:, HALF:]


def finish(t_ref, f_ref, index, c, buf_ref):
    at = c * ROWS if isinstance(c, int) else pl.multiple_of(c * ROWS, ROWS)
    v = jnp.concatenate([t_ref[h, pl.ds(at, ROWS), :] for h in range(2)], axis=1)
    buf_ref[c] = (f_ref[index, c].astype(F32) + v).astype(BF16)


def out_copy(buf_ref, out_ref, index, part, sems):
    span = pl.ds(part * (C // PARTS), C // PARTS)
    return pltpu.make_async_copy(buf_ref.at[span], out_ref.at[index, span], sems.at[part])


def own_last(
    a1_ref, raw0_ref, w1_ref, w2_any, gain_any, gain2_any, frames_any,
    a0_ref, o1_ref, wt1_ref, w2_ref, m_ref, g2_ref,
    gain_ref, gain2_ref, frames_ref, t_ref, x_ref, sems,
):
    small = [
        pltpu.make_async_copy(src, dst, sems.at[i])
        for i, (src, dst) in enumerate(
            ((gain_any, gain_ref), (frames_any, frames_ref), (gain2_any, gain2_ref))
        )
    ]
    third = DEPTH
    loads = [
        pltpu.make_async_copy(
            w2_any.at[pl.ds(k * third, third)], w2_ref.at[pl.ds(k * third, third)], sems.at[3 + k]
        )
        for k in range(TAPS)
    ]
    for copy in small + loads:
        copy.start()
    for step in turn_pieces(w1_ref, wt1_ref, (0,)):
        step()
    clear_edges(x_ref)
    put(x_ref, a1_ref, 0)
    put(x_ref, a1_ref, 1)
    inverse = [inverse_rms(raw0_ref, h) for h in range(2)]
    for copy in small:
        copy.wait()
    masks = tap_masks(frames_ref)
    for i in range(8):
        m_ref[i : i + 1, :] = jnp.full((1, COLS), masks[i % 4], F32)
    later = turn_pieces(w1_ref, wt1_ref, (1, 2))
    share = C // ROWS
    for row in range(ROWS):
        d = product(wt1_ref, 0, 1, x_ref, row)
        put(x_ref, a1_ref, row + 2)
        for c in range(row * share, (row + 1) * share):
            for h in range(2):
                activate(raw0_ref, h, c, inverse[h], gain_ref, t_ref)
            g2_ref[c : c + 1, :] = jnp.full((1, COLS), gain2_ref[c], F32)
        for step in later[row * len(later) // ROWS : (row + 1) * len(later) // ROWS]:
            step()
        o1_ref[row] = d
    for h in range(2):
        to_rows(t_ref, h, a0_ref)
    for load in loads:
        load.wait()


def own_first(a0_ref, o1_ref, wt1_ref, w2_ref, m_ref, p0_ref, p1_ref, wt2_ref, x_ref):
    clear_edges(x_ref)
    put(x_ref, a0_ref, 0)
    put(x_ref, a0_ref, 1)
    later = turn_pieces(w2_ref, wt2_ref, (0, 1, 2))
    for row in range(ROWS):
        d = product(wt1_ref, 0, 2, x_ref, row)
        put(x_ref, a0_ref, row + 2)
        for step in later[row * len(later) // ROWS : (row + 1) * len(later) // ROWS]:
            step()
        p0_ref[row] = d[:C]
        p1_ref[row] = o1_ref[row] + mask(m_ref, 2) * d[C:]


def halo_first(h_ref, o1_ref, wt_ref, g_ref, m_ref, s_ref, x_ref):
    clear_edges(x_ref)
    put(x_ref, h_ref, 0)
    put(x_ref, h_ref, 1)
    for row in range(ROWS):
        d = product(wt_ref, 2, 3, x_ref, row)
        put(x_ref, h_ref, row + 2)
        s_ref[row] = second_activation(o1_ref[row] + mask(m_ref, 3) * d, g_ref)


def halo_middle(o0_ref, x_ref, wt_ref, m_ref, p_ref):
    for row in range(ROWS):
        p_ref[row] = o0_ref[row] + mask(m_ref, 0) * product(wt_ref, 1, 2, x_ref, row)


def halo_second(h_ref, p_ref, wt_ref, g_ref, m_ref, s_ref, x_ref):
    clear_edges(x_ref)
    put(x_ref, h_ref, 0)
    put(x_ref, h_ref, 1)
    for row in range(ROWS):
        d = product(wt_ref, 2, 3, x_ref, row)
        put(x_ref, h_ref, row + 2)
        s_ref[row] = second_activation(p_ref[row] + mask(m_ref, 1) * d, g_ref)


def local_second(s0_ref, s1_ref, wt_ref, m_ref, o0_ref, o1_ref, x0_ref, x1_ref):
    clear_edges(x0_ref)
    put(x0_ref, s0_ref, 0)
    put(x0_ref, s0_ref, 1)
    for row in range(ROWS):
        d = product(wt_ref, 0, 2, x0_ref, row)
        put(x0_ref, s0_ref, row + 2)
        put(x1_ref, s1_ref, row)
        o0_ref[row] = d[:C]
        o1_ref[row] = mask(m_ref, 2) * d[C:]
    clear_edges(x1_ref)
    for row in range(ROWS):
        o1_ref[row] += product(wt_ref, 0, 1, x1_ref, row)


def last_frame(h_ref, o0_ref, o1_ref, wt_ref, m_ref, p_ref, t_ref, x_ref):
    clear_edges(x_ref)
    put(x_ref, h_ref, 0)
    put(x_ref, h_ref, 1)
    for row in range(ROWS):
        d = product(wt_ref, 1, 3, x_ref, row)
        put(x_ref, h_ref, row + 2)
        p_ref[row] = o0_ref[row] + mask(m_ref, 0) * d[:C]
        put_transposed(t_ref, row, o1_ref[row] + mask(m_ref, 3) * d[C:])


def other_frame(
    h_ref, p_ref, wt_ref, m_ref, t1_ref, f_ref, out_ref, t_ref, x_ref, buf0_ref, buf1_ref, sems0, sems1
):
    clear_edges(x_ref)
    put(x_ref, h_ref, 0)
    put(x_ref, h_ref, 1)
    share = C // ROWS
    for row in range(ROWS):
        d = product(wt_ref, 2, 3, x_ref, row)
        put(x_ref, h_ref, row + 2)
        for c in range(row * share, (row + 1) * share):
            finish(t1_ref, f_ref, 1, c, buf1_ref)
        put_transposed(t_ref, row, p_ref[row] + mask(m_ref, 1) * d)
        if (row + 1) % (ROWS // PARTS) == 0:
            out_copy(buf1_ref, out_ref, 1, row // (ROWS // PARTS), sems1).start()
    for part in range(PARTS):

        def step(b, _):
            for j in range(16):
                finish(t_ref, f_ref, 0, part * (C // PARTS) + b * 16 + j, buf0_ref)
            return 0

        lax.fori_loop(0, C // PARTS // 16, step, 0)
        out_copy(buf0_ref, out_ref, 0, part, sems0).start()
    for part in range(PARTS):
        out_copy(buf1_ref, out_ref, 1, part, sems1).wait()
        out_copy(buf0_ref, out_ref, 0, part, sems0).wait()


VM = pl.BlockSpec(memory_space=pltpu.VMEM)
ANY = pl.BlockSpec(memory_space=pl.ANY)
HBM = pl.BlockSpec(memory_space=pltpu.HBM)
NATURAL = pltpu.VMEM((2, C * ROWS, HALF), F32)
RAW = pltpu.VMEM((2, C, ROWS, HALF), BF16)
SLABS = pltpu.VMEM(((ROWS + 2) * SLAB, COLS), BF16)
FRAME = pltpu.VMEM((C, ROWS, COLS), BF16)
GAIN = pltpu.SMEM((C,), F32)
SEMS = pltpu.SemaphoreType.DMA((PARTS,))
A_SUM = jax.ShapeDtypeStruct((ROWS, C, COLS), F32)
A_ACT = jax.ShapeDtypeStruct((ROWS, C, COLS), BF16)
A_RAW = jax.ShapeDtypeStruct((2, C, ROWS, HALF), BF16)
A_SLABS = jax.ShapeDtypeStruct(((ROWS + 2) * SLAB, COLS), BF16)
A_NATURAL = jax.ShapeDtypeStruct((2, C * ROWS, HALF), F32)
A_WEIGHTS = jax.ShapeDtypeStruct((TAPS * DEPTH, C), BF16)
A_TURNED = jax.ShapeDtypeStruct((TAPS * C, DEPTH), BF16)
A_MASKS = jax.ShapeDtypeStruct((8, COLS), F32)
A_GAINS = jax.ShapeDtypeStruct((C, COLS), F32)


def stay(value):
    return pltpu.with_memory_space_constraint(value, pltpu.HBM)


def call(kernel, in_specs, out_shape, scratch=(), out_specs=None):
    return pl.pallas_call(
        kernel,
        in_specs=in_specs,
        out_specs=out_specs or jax.tree.map(lambda _: VM, out_shape),
        out_shape=out_shape,
        scratch_shapes=scratch,
        compiler_params=pltpu.CompilerParams(vmem_limit_bytes=VMEM_LIMIT),
        name=kernel.__name__,
    )


def per_device(features, video_frames, gain_first, conv_first, gain_second, conv_second):
    w1 = conv_first.reshape(TAPS * DEPTH, C)
    w2 = conv_second.reshape(TAPS * DEPTH, C)

    a1, raw0 = call(
        activate_last, [HBM, HBM], [A_ACT, A_RAW],
        [RAW, GAIN, NATURAL, pltpu.SemaphoreType.DMA((5,)), pltpu.SemaphoreType.DMA((4,))],
    )(stay(features), stay(gain_first))
    a_before = shifted(a1, "tm")
    a0, o1, wt1, w2, m, g2 = call(
        own_last, [VM] * 3 + [HBM] * 4, [A_ACT, A_SUM, A_TURNED, A_WEIGHTS, A_MASKS, A_GAINS],
        [
            GAIN, GAIN, pltpu.SMEM(video_frames.shape, jnp.int32), NATURAL, SLABS,
            pltpu.SemaphoreType.DMA((6,)),
        ],
    )(a1, raw0, w1, stay(w2), stay(gain_first), stay(gain_second), stay(video_frames))
    a_earlier = shifted(a0, "tm")
    p0, p1, wt2 = call(own_first, [VM] * 5, [A_SUM, A_SUM, A_TURNED], [SLABS])(a0, o1, wt1, w2, m)
    s1, x = call(halo_first, [VM] * 5, [A_ACT, A_SLABS])(a_before, p1, wt1, g2, m)
    s_before = shifted(s1, "tm")
    part = call(halo_middle, [VM] * 4, A_SUM)(p0, x, wt1, m)
    s0 = call(halo_second, [VM] * 5, A_ACT, [SLABS])(a_earlier, part, wt1, g2, m)
    s_earlier = shifted(s0, "tm")
    q0, q1 = call(local_second, [VM] * 4, [A_SUM, A_SUM], [SLABS, SLABS])(s0, s1, wt2, m)
    part2, t1 = call(last_frame, [VM] * 5, [A_SUM, A_NATURAL], [SLABS])(s_before, q0, q1, wt2, m)
    return call(
        other_frame, [VM] * 6, jax.ShapeDtypeStruct(features.shape, BF16),
        [NATURAL, SLABS, FRAME, FRAME, SEMS, SEMS], out_specs=ANY,
    )(s_earlier, part2, wt2, m, t1, features)


def solution(mesh):
    in_specs = (P(("group", "tm"), None, None, None), P("group"), P(), P(), P(), P())
    out_specs = P(("group", "tm"), None, None, None)
    return jax.shard_map(
        per_device, mesh=mesh, in_specs=in_specs, out_specs=out_specs, check_vma=False
    )
```

```python
import jax
import jax.numpy as jnp
from jax import lax
from jax.experimental import pallas as pl
from jax.experimental.pallas import tpu as pltpu
from jax.sharding import PartitionSpec as P

C = 192
ROWS = 8
COLS = 256
HALF = 128
TAPS = 3
SLAB = 3 * C
DEPTH = 9 * C
PIECE = 384
PARTS = 4
EARLY = 6
EPS = 1e-06
VMEM_LIMIT = 16 * 1024 * 1024
F32 = jnp.float32
BF16 = jnp.bfloat16


def shifted(value, axis):
    count = lax.axis_size(axis)
    return lax.ppermute(value, axis, [(i, i + 1) for i in range(count - 1)])


def tap_masks(frames_ref):
    first = 2 * lax.axis_index("tm")

    def step(v, carry):
        begin, start0, start1 = carry
        start0 = jnp.where(begin <= first, begin, start0)
        start1 = jnp.where(begin <= first + 1, begin, start1)
        return begin + frames_ref[v], start0, start1

    zero = jnp.int32(0)
    _, start0, start1 = lax.fori_loop(0, frames_ref.shape[0], step, (zero, zero, zero))
    return tuple(
        jnp.where(test, 1.0, 0.0).astype(F32)
        for test in (
            first - 1 >= start0,
            first - 2 >= start0,
            first >= start1,
            first - 1 >= start1,
        )
    )


def mask(m_ref, i):
    return m_ref[i : i + 1, :]


def turn_pieces(w_ref, wt_ref, taps, start=0):
    def turn(k, lo, hi):
        base = (k - start) * DEPTH
        wt_ref[k * C : (k + 1) * C, lo:hi] = w_ref[base + lo : base + hi, :].T

    return [
        (lambda k=k, lo=lo: turn(k, lo, min(lo + PIECE, DEPTH)))
        for k in taps
        for lo in range(0, DEPTH, PIECE)
    ]


def put_row(x_ref, row, values):
    base = (row + 1) * SLAB
    cols = lax.broadcasted_iota(jnp.int32, (C, COLS), 1)
    left = jnp.where(cols == 0, 0.0, pltpu.roll(values, 1, 1))
    right = jnp.where(cols == COLS - 1, 0.0, pltpu.roll(values, COLS - 1, 1))
    x_ref[base : base + C, :] = left.astype(BF16)
    x_ref[base + C : base + 2 * C, :] = values.astype(BF16)
    x_ref[base + 2 * C : base + 3 * C, :] = right.astype(BF16)


def clear_edges(x_ref):
    zeros = jnp.zeros((SLAB, COLS), BF16)
    x_ref[0:SLAB, :] = zeros
    x_ref[(ROWS + 1) * SLAB : (ROWS + 2) * SLAB, :] = zeros


def put(x_ref, a_ref, row, start=0):
    if row - start < a_ref.shape[0]:
        put_row(x_ref, row, a_ref[row - start].astype(F32))


def product(wt_ref, lo, hi, x_ref, row):
    return jnp.dot(
        wt_ref[lo * C : hi * C, :],
        x_ref[row * SLAB : row * SLAB + DEPTH, :],
        preferred_element_type=F32,
    )


def inverse_rms(raw_ref, h):
    def squares(b, total):
        v = raw_ref[h, pl.ds(b * 16, 16)].astype(F32)
        return total + jnp.sum(v * v, axis=0)

    total = lax.fori_loop(0, C // 16, squares, jnp.zeros((ROWS, HALF), F32))
    return lax.rsqrt(total * (1.0 / C) + EPS)


def activate(raw_ref, h, c, inverse, gain_ref, t_ref):
    u = raw_ref[h, c].astype(F32) * inverse * gain_ref[c]
    at = c * ROWS if isinstance(c, int) else pl.multiple_of(c * ROWS, ROWS)
    t_ref[h, pl.ds(at, ROWS), :] = u * jax.nn.sigmoid(u)


def to_rows(t_ref, h, a_ref):
    for row in range(ROWS):
        a_ref[row, :, h * HALF : (h + 1) * HALF] = t_ref[
            h, pl.ds(row, C, stride=ROWS), :
        ].astype(BF16)


def frame_copies(f_ref, index, raw_ref, sems):
    return [
        [
            pltpu.make_async_copy(
                f_ref.at[index, pl.ds(q * C // 2, C // 2), :, pl.ds(h * HALF, HALF)],
                raw_ref.at[h, pl.ds(q * C // 2, C // 2)],
                sems.at[2 * h + q],
            )
            for q in range(2)
        ]
        for h in range(2)
    ]


def activate_last(
    f_ref, w1_any, gain_any, a_ref, raw0_ref, w_ref, raw1_ref, gain_ref, t_ref, sems, sems0
):
    copies = frame_copies(f_ref, 1, raw1_ref, sems)
    others = frame_copies(f_ref, 0, raw0_ref, sems0)
    gains = pltpu.make_async_copy(gain_any, gain_ref, sems.at[4])
    later = [pltpu.make_async_copy(w1_any.at[pl.ds(0, DEPTH)], w_ref, sems.at[5])] + others[0] + others[1]
    for copy in copies[0] + [gains] + copies[1] + later:
        copy.start()
    for h in range(2):
        for copy in copies[h]:
            copy.wait()
        inverse = inverse_rms(raw1_ref, h)
        if h == 0:
            gains.wait()

        for c in range(C):
            activate(raw1_ref, h, c, inverse, gain_ref, t_ref)
        to_rows(t_ref, h, a_ref)
    for copy in later:
        copy.wait()


def second_activation(values, g_ref):
    mean_square = jnp.sum(values * values, axis=0, keepdims=True) * (1.0 / C)
    u = values * lax.rsqrt(mean_square + EPS) * g_ref[...]
    return (u * jax.nn.sigmoid(u)).astype(BF16)


def put_transposed(t_ref, row, values):
    t_ref[0, pl.ds(row, C, stride=ROWS), :] = values[:, :HALF]
    t_ref[1, pl.ds(row, C, stride=ROWS), :] = values[:, HALF:]


def finish(t_ref, f_ref, index, c, buf_ref):
    at = c * ROWS if isinstance(c, int) else pl.multiple_of(c * ROWS, ROWS)
    v = jnp.concatenate([t_ref[h, pl.ds(at, ROWS), :] for h in range(2)], axis=1)
    buf_ref[c] = (f_ref[index, c].astype(F32) + v).astype(BF16)


def out_copy(buf_ref, out_ref, index, part, sems):
    span = pl.ds(part * (C // PARTS), C // PARTS)
    return pltpu.make_async_copy(buf_ref.at[span], out_ref.at[index, span], sems.at[part])


def own_last(
    a1_ref, raw0_ref, first_ref, w1_any, w2_any, gain_any, gain2_any, frames_any,
    a0_ref, o1_ref, wt1_ref, w2_ref, m_ref, g2_ref,
    gain_ref, gain2_ref, frames_ref, t_ref, x_ref, w1_ref, sems,
):
    small = [
        pltpu.make_async_copy(src, dst, sems.at[i])
        for i, (src, dst) in enumerate(
            ((gain_any, gain_ref), (frames_any, frames_ref), (gain2_any, gain2_ref))
        )
    ]
    others = pltpu.make_async_copy(w1_any.at[pl.ds(DEPTH, 2 * DEPTH)], w1_ref, sems.at[3])
    load = pltpu.make_async_copy(w2_any, w2_ref, sems.at[4])
    for copy in small + [others, load]:
        copy.start()
    for step in turn_pieces(first_ref, wt1_ref, (0,)):
        step()
    clear_edges(x_ref)
    put(x_ref, a1_ref, 0)
    put(x_ref, a1_ref, 1)
    inverse = [inverse_rms(raw0_ref, h) for h in range(2)]
    for copy in small:
        copy.wait()
    masks = tap_masks(frames_ref)
    for i in range(8):
        m_ref[i : i + 1, :] = jnp.full((1, COLS), masks[i % 4], F32)
    later = turn_pieces(w1_ref, wt1_ref, (1, 2), 1)
    share = C // ROWS
    for row in range(ROWS):
        d = product(wt1_ref, 0, 1, x_ref, row)
        put(x_ref, a1_ref, row + 2)
        for c in range(row * share, (row + 1) * share):
            for h in range(2):
                activate(raw0_ref, h, c, inverse[h], gain_ref, t_ref)
            g2_ref[c : c + 1, :] = jnp.full((1, COLS), gain2_ref[c], F32)
        if row == 2:
            others.wait()
        if row >= 2:
            for step in later[(row - 2) * len(later) // 6 : (row - 1) * len(later) // 6]:
                step()
        o1_ref[row] = d
    for h in range(2):
        to_rows(t_ref, h, a0_ref)
    load.wait()


def own_first(a0_ref, o1_ref, wt1_ref, w2_ref, m_ref, p0_ref, p1_ref, wt2_ref, x_ref):
    clear_edges(x_ref)
    put(x_ref, a0_ref, 0)
    put(x_ref, a0_ref, 1)
    later = turn_pieces(w2_ref, wt2_ref, (0, 1, 2))
    for row in range(ROWS):
        d = product(wt1_ref, 0, 2, x_ref, row)
        put(x_ref, a0_ref, row + 2)
        for step in later[row * len(later) // ROWS : (row + 1) * len(later) // ROWS]:
            step()
        p0_ref[row] = d[:C]
        p1_ref[row] = o1_ref[row] + mask(m_ref, 2) * d[C:]


def halo_first(h_ref, o1_ref, wt_ref, g_ref, m_ref, s_ref, x_ref):
    clear_edges(x_ref)
    put(x_ref, h_ref, 0)
    put(x_ref, h_ref, 1)
    for row in range(ROWS):
        d = product(wt_ref, 2, 3, x_ref, row)
        put(x_ref, h_ref, row + 2)
        s_ref[row] = second_activation(o1_ref[row] + mask(m_ref, 3) * d, g_ref)


def halo_middle(o0_ref, x_ref, wt1_ref, m_ref, s1_ref, wt2_ref, p_ref, q_ref, x1_ref):
    clear_edges(x1_ref)
    for row in range(ROWS):
        p_ref[row] = o0_ref[row] + mask(m_ref, 0) * product(wt1_ref, 1, 2, x_ref, row)
        put(x1_ref, s1_ref, row)
    for row in range(ROWS):
        q_ref[row] = product(wt2_ref, 0, 1, x1_ref, row)


def halo_second(h_ref, p_ref, wt_ref, g_ref, m_ref, s_ref, end_ref, x_ref):
    clear_edges(x_ref)
    put(x_ref, h_ref, 0)
    put(x_ref, h_ref, 1)
    for row in range(ROWS):
        d = product(wt_ref, 2, 3, x_ref, row)
        put(x_ref, h_ref, row + 2)
        act = second_activation(p_ref[row] + mask(m_ref, 1) * d, g_ref)
        if row < EARLY:
            s_ref[row] = act
        else:
            end_ref[row - EARLY] = act


def local_second(s0_ref, end_ref, p_ref, wt_ref, m_ref, o0_ref, o1_ref, x_ref):
    clear_edges(x_ref)
    put(x_ref, s0_ref, 0)
    put(x_ref, s0_ref, 1)
    for row in range(ROWS):
        d = product(wt_ref, 0, 2, x_ref, row)
        if row + 2 < EARLY:
            put(x_ref, s0_ref, row + 2)
        else:
            put(x_ref, end_ref, row + 2, EARLY)
        o0_ref[row] = d[:C]
        o1_ref[row] = p_ref[row] + mask(m_ref, 2) * d[C:]


def last_frame(h_ref, o0_ref, o1_ref, wt_ref, m_ref, p_ref, t_ref, x_ref):
    clear_edges(x_ref)
    put(x_ref, h_ref, 0)
    put(x_ref, h_ref, 1)
    for row in range(ROWS):
        d = product(wt_ref, 1, 3, x_ref, row)
        put(x_ref, h_ref, row + 2)
        p_ref[row] = o0_ref[row] + mask(m_ref, 0) * d[:C]
        put_transposed(t_ref, row, o1_ref[row] + mask(m_ref, 3) * d[C:])


def early_rows(h_ref, p_ref, wt_ref, m_ref, t1_ref, f_ref, t_ref, x_ref, out_ref, buf_ref, sems):
    clear_edges(x_ref)
    put(x_ref, h_ref, 0)
    put(x_ref, h_ref, 1)
    rows = EARLY - 1
    for row in range(rows):
        d = product(wt_ref, 2, 3, x_ref, row)
        put(x_ref, h_ref, row + 2)
        for c in range(row * C // rows, (row + 1) * C // rows):
            finish(t1_ref, f_ref, 1, c, buf_ref)
        put_transposed(t_ref, row, p_ref[row] + mask(m_ref, 1) * d)
        for part in range(PARTS):
            if row * C // rows < (part + 1) * C // PARTS <= (row + 1) * C // rows:
                out_copy(buf_ref, out_ref, 1, part, sems).start()
    for part in range(PARTS):
        out_copy(buf_ref, out_ref, 1, part, sems).wait()


def late_rows(
    end_ref, p_ref, wt_ref, m_ref, f_ref, _, __, ___, t_ref, x_ref, out_ref, buf_ref, sems
):
    for row in range(EARLY, ROWS):
        put(x_ref, end_ref, row, EARLY)
    for row in range(EARLY - 1, ROWS):
        d = product(wt_ref, 2, 3, x_ref, row)
        put_transposed(t_ref, row, p_ref[row] + mask(m_ref, 1) * d)
    for part in range(PARTS):

        def step(b, _):
            for j in range(16):
                finish(t_ref, f_ref, 0, part * (C // PARTS) + b * 16 + j, buf_ref)
            return 0

        lax.fori_loop(0, C // PARTS // 16, step, 0)
        out_copy(buf_ref, out_ref, 0, part, sems).start()
    for part in range(PARTS):
        out_copy(buf_ref, out_ref, 0, part, sems).wait()


VM = pl.BlockSpec(memory_space=pltpu.VMEM)
ANY = pl.BlockSpec(memory_space=pl.ANY)
HBM = pl.BlockSpec(memory_space=pltpu.HBM)
NATURAL = pltpu.VMEM((2, C * ROWS, HALF), F32)
RAW = pltpu.VMEM((2, C, ROWS, HALF), BF16)
SLABS = pltpu.VMEM(((ROWS + 2) * SLAB, COLS), BF16)
FRAME = pltpu.VMEM((C, ROWS, COLS), BF16)
GAIN = pltpu.SMEM((C,), F32)
SEMS = pltpu.SemaphoreType.DMA((PARTS,))
A_SUM = jax.ShapeDtypeStruct((ROWS, C, COLS), F32)
A_ACT = jax.ShapeDtypeStruct((ROWS, C, COLS), BF16)
A_EARLY = jax.ShapeDtypeStruct((EARLY, C, COLS), BF16)
A_LATE = jax.ShapeDtypeStruct((ROWS - EARLY, C, COLS), BF16)
A_FIRST = jax.ShapeDtypeStruct((DEPTH, C), BF16)
A_RAW = jax.ShapeDtypeStruct((2, C, ROWS, HALF), BF16)
A_SLABS = jax.ShapeDtypeStruct(((ROWS + 2) * SLAB, COLS), BF16)
A_NATURAL = jax.ShapeDtypeStruct((2, C * ROWS, HALF), F32)
A_WEIGHTS = jax.ShapeDtypeStruct((TAPS * DEPTH, C), BF16)
A_TURNED = jax.ShapeDtypeStruct((TAPS * C, DEPTH), BF16)
A_MASKS = jax.ShapeDtypeStruct((8, COLS), F32)
A_GAINS = jax.ShapeDtypeStruct((C, COLS), F32)


def stay(value):
    return pltpu.with_memory_space_constraint(value, pltpu.HBM)


def call(kernel, in_specs, out_shape, scratch=(), out_specs=None, aliases=None):
    return pl.pallas_call(
        kernel,
        in_specs=in_specs,
        out_specs=out_specs or jax.tree.map(lambda _: VM, out_shape),
        out_shape=out_shape,
        scratch_shapes=scratch,
        input_output_aliases=aliases or {},
        compiler_params=pltpu.CompilerParams(vmem_limit_bytes=VMEM_LIMIT),
        name=kernel.__name__,
    )


def per_device(features, video_frames, gain_first, conv_first, gain_second, conv_second):
    w1 = conv_first.reshape(TAPS * DEPTH, C)
    w2 = conv_second.reshape(TAPS * DEPTH, C)

    a1, raw0, first = call(
        activate_last, [HBM] * 3, [A_ACT, A_RAW, A_FIRST],
        [RAW, GAIN, NATURAL, pltpu.SemaphoreType.DMA((6,)), pltpu.SemaphoreType.DMA((4,))],
    )(stay(features), stay(w1), stay(gain_first))
    a_before = shifted(a1, "tm")
    a0, o1, wt1, w2, m, g2 = call(
        own_last, [VM] * 3 + [HBM] * 5, [A_ACT, A_SUM, A_TURNED, A_WEIGHTS, A_MASKS, A_GAINS],
        [
            GAIN, GAIN, pltpu.SMEM(video_frames.shape, jnp.int32), NATURAL, SLABS,
            pltpu.VMEM((2 * DEPTH, C), BF16), pltpu.SemaphoreType.DMA((5,)),
        ],
    )(a1, raw0, first, stay(w1), stay(w2), stay(gain_first), stay(gain_second), stay(video_frames))
    a_earlier = shifted(a0, "tm")
    p0, p1, wt2 = call(own_first, [VM] * 5, [A_SUM, A_SUM, A_TURNED], [SLABS])(a0, o1, wt1, w2, m)
    s1, x = call(halo_first, [VM] * 5, [A_ACT, A_SLABS])(a_before, p1, wt1, g2, m)
    s_before = shifted(s1, "tm")
    part, q = call(halo_middle, [VM] * 6, [A_SUM, A_SUM], [SLABS])(p0, x, wt1, m, s1, wt2)
    s0, end = call(halo_second, [VM] * 5, [A_EARLY, A_LATE], [SLABS])(a_earlier, part, wt1, g2, m)
    s_earlier = shifted(s0, "tm")
    s_end = shifted(end, "tm")
    q0, q1 = call(local_second, [VM] * 5, [A_SUM, A_SUM], [SLABS])(s0, end, q, wt2, m)
    part2, t1 = call(last_frame, [VM] * 5, [A_SUM, A_NATURAL], [SLABS])(s_before, q0, q1, wt2, m)
    whole = jax.ShapeDtypeStruct(features.shape, BF16)
    t0, x0, out = call(
        early_rows, [VM] * 6, [A_NATURAL, A_SLABS, whole], [FRAME, SEMS], [VM, VM, ANY]
    )(s_earlier, part2, wt2, m, t1, features)
    return call(
        late_rows, [VM] * 7 + [ANY], [A_NATURAL, A_SLABS, whole], [FRAME, SEMS], [VM, VM, ANY],
        {5: 0, 6: 1, 7: 2},
    )(s_end, part2, wt2, m, features, t0, x0, out)[2]


def solution(mesh):
    in_specs = (P(("group", "tm"), None, None, None), P("group"), P(), P(), P(), P())
    out_specs = P(("group", "tm"), None, None, None)
    return jax.shard_map(
        per_device, mesh=mesh, in_specs=in_specs, out_specs=out_specs, check_vma=False
    )
```

```python
import jax
import jax.numpy as jnp
from jax import lax
from jax.experimental import pallas as pl
from jax.experimental.pallas import tpu as pltpu
from jax.sharding import PartitionSpec as P

C = 192
ROWS = 8
COLS = 256
HALF = 128
TAPS = 3
SLAB = 3 * C
DEPTH = 9 * C
PIECE = 384
PARTS = 4
EPS = 1e-06
VMEM_LIMIT = 18 * 1024 * 1024
F32 = jnp.float32
BF16 = jnp.bfloat16


def shifted(value):
    return lax.ppermute(value, "tm", [(i, i + 1) for i in range(lax.axis_size("tm") - 1)])


def to_next_pair(value):
    return lax.ppermute(value, "tm", [(i, i + 1) for i in range(1, lax.axis_size("tm") - 1, 2)])


def within_pair(value):
    return lax.ppermute(value, "tm", [(i, i + 1) for i in range(0, lax.axis_size("tm"), 2)])


def tap_masks(frames_ref):
    first = 2 * lax.axis_index("tm")

    def step(v, carry):
        begin, start0, start1 = carry
        start0 = jnp.where(begin <= first, begin, start0)
        start1 = jnp.where(begin <= first + 1, begin, start1)
        return begin + frames_ref[v], start0, start1

    zero = jnp.int32(0)
    _, start0, start1 = lax.fori_loop(0, frames_ref.shape[0], step, (zero, zero, zero))
    return tuple(
        jnp.where(test, 1.0, 0.0).astype(F32)
        for test in (
            first - 1 >= start0,
            first - 2 >= start0,
            first >= start1,
            first - 1 >= start1,
        )
    )


def mask(m_ref, i):
    return m_ref[i : i + 1, :]


def turn_pieces(w_ref, wt_ref, taps, start=0):
    def turn(k, lo, hi):
        base = (k - start) * DEPTH
        wt_ref[k * C : (k + 1) * C, lo:hi] = w_ref[base + lo : base + hi, :].T

    return [
        (lambda k=k, lo=lo: turn(k, lo, min(lo + PIECE, DEPTH)))
        for k in taps
        for lo in range(0, DEPTH, PIECE)
    ]


def put_row(x_ref, row, values):
    base = (row + 1) * SLAB
    cols = lax.broadcasted_iota(jnp.int32, (C, COLS), 1)
    left = jnp.where(cols == 0, 0.0, pltpu.roll(values, 1, 1))
    right = jnp.where(cols == COLS - 1, 0.0, pltpu.roll(values, COLS - 1, 1))
    x_ref[base : base + C, :] = left.astype(BF16)
    x_ref[base + C : base + 2 * C, :] = values.astype(BF16)
    x_ref[base + 2 * C : base + 3 * C, :] = right.astype(BF16)


def clear_edges(x_ref):
    zeros = jnp.zeros((SLAB, COLS), BF16)
    x_ref[0:SLAB, :] = zeros
    x_ref[(ROWS + 1) * SLAB : (ROWS + 2) * SLAB, :] = zeros


def put(x_ref, a_ref, row):
    if row < ROWS:
        put_row(x_ref, row, a_ref[row].astype(F32))


def put_either(x_ref, far_ref, near_ref, row):
    if row < ROWS:
        put_row(x_ref, row, far_ref[row].astype(F32) + near_ref[row].astype(F32))


def product(wt_ref, lo, hi, x_ref, row):
    return jnp.dot(
        wt_ref[lo * C : hi * C, :],
        x_ref[row * SLAB : row * SLAB + DEPTH, :],
        preferred_element_type=F32,
    )


def sends_far():
    return lax.rem(lax.axis_index("tm"), 2) == 1


def inverse_rms(raw_ref, h):
    cols = slice(h * HALF, (h + 1) * HALF)

    def squares(b, total):
        v = raw_ref[pl.ds(b * 16, 16), :, cols].astype(F32)
        return total + jnp.sum(v * v, axis=0)

    total = lax.fori_loop(0, C // 16, squares, jnp.zeros((ROWS, HALF), F32))
    return lax.rsqrt(total * (1.0 / C) + EPS)


def activate(raw_ref, h, c, inverse, gain, t_ref):
    u = raw_ref[c, :, h * HALF : (h + 1) * HALF].astype(F32) * inverse * gain
    t_ref[h, c * ROWS : (c + 1) * ROWS, :] = u * jax.nn.sigmoid(u)


def row_of(t_ref, h, row):
    return t_ref[h, pl.ds(row, C, stride=ROWS), :]


def to_rows(t_ref, h, a_ref):
    for row in range(ROWS):
        a_ref[row, :, h * HALF : (h + 1) * HALF] = row_of(t_ref, h, row).astype(BF16)


def frame_copies(f_ref, index, raw_ref, sems):
    return [
        [
            pltpu.make_async_copy(
                f_ref.at[index, pl.ds(q * C // 2, C // 2), :, pl.ds(h * HALF, HALF)],
                raw_ref.at[pl.ds(q * C // 2, C // 2), :, pl.ds(h * HALF, HALF)],
                sems.at[2 * h + q],
            )
            for q in range(2)
        ]
        for h in range(2)
    ]


def first_tap(w1_any, w_ref, sem):
    return pltpu.make_async_copy(w1_any.at[pl.ds(0, DEPTH)], w_ref, sem)


def flat(copies):
    return copies[0] + copies[1]


def activate_frame(raw_ref, gain, t_ref, a_ref, before=None, extra=None):
    for h in range(2):
        if before:
            before(h)
        inverse = inverse_rms(raw_ref, h)
        for c in range(C):
            activate(raw_ref, h, c, inverse, gain(c), t_ref)
            if extra and h == 0:
                extra(c)
        to_rows(t_ref, h, a_ref)


def waits(copies):
    def wait(h):
        for copy in copies[h]:
            copy.wait()

    return wait


def first_sent(
    f_ref, w1_any, gain_any, a_ref, raw0_ref, w_ref, g1_ref, raw1_ref, gain_ref, t_ref, sems, sems0
):
    @pl.when(sends_far())
    def _():
        copies = frame_copies(f_ref, 1, raw1_ref, sems)
        gains = pltpu.make_async_copy(gain_any, gain_ref, sems.at[4])
        later = [first_tap(w1_any, w_ref, sems.at[5])] + flat(frame_copies(f_ref, 0, raw0_ref, sems0))
        for copy in copies[0] + [gains] + copies[1] + later:
            copy.start()

        def before(h):
            waits(copies)(h)
            if h == 0:
                gains.wait()

        def spread(c):
            g1_ref[c : c + 1, :] = jnp.full((1, HALF), gain_ref[c], F32)

        activate_frame(raw1_ref, lambda c: gain_ref[c], t_ref, a_ref, before, spread)
        for copy in later:
            copy.wait()


def rest_sent(
    a_ref, raw0_ref, g1_ref, _, f_ref, w1_any, gain_any,
    first_ref, a0_ref, a1_ref, gain_ref, raw_ref, last_ref, t_ref, sems, sems0, sems1,
):
    far = sends_far()

    @pl.when(far)
    def _():
        a1_ref[...] = a_ref[...]
        activate_frame(raw0_ref, lambda c: g1_ref[c : c + 1, :], t_ref, a0_ref)

    @pl.when(jnp.logical_not(far))
    def _():
        gains = pltpu.make_async_copy(gain_any, gain_ref, sems.at[0])
        first = first_tap(w1_any, first_ref, sems.at[1])
        last = frame_copies(f_ref, 1, last_ref, sems1)
        other = frame_copies(f_ref, 0, raw_ref, sems0)
        for copy in last[0] + [gains] + last[1] + flat(other) + [first]:
            copy.start()
        gains.wait()
        activate_frame(last_ref, lambda c: gain_ref[c], t_ref, a1_ref, waits(last))
        activate_frame(raw_ref, lambda c: gain_ref[c], t_ref, a0_ref, waits(other))
        first.wait()


def second_activation(values, g_ref):
    mean_square = jnp.sum(values * values, axis=0, keepdims=True) * (1.0 / C)
    u = values * lax.rsqrt(mean_square + EPS) * g_ref[...]
    return (u * jax.nn.sigmoid(u)).astype(BF16)


def put_transposed(t_ref, row, values):
    t_ref[0, pl.ds(row, C, stride=ROWS), :] = values[:, :HALF]
    t_ref[1, pl.ds(row, C, stride=ROWS), :] = values[:, HALF:]


def finish(t_ref, f_ref, index, c, buf_ref):
    at = c * ROWS if isinstance(c, int) else pl.multiple_of(c * ROWS, ROWS)
    v = jnp.concatenate([t_ref[h, pl.ds(at, ROWS), :] for h in range(2)], axis=1)
    buf_ref[c] = (f_ref[index, c].astype(F32) + v).astype(BF16)


def out_copy(buf_ref, out_ref, index, part, sems):
    span = pl.ds(part * (C // PARTS), C // PARTS)
    return pltpu.make_async_copy(buf_ref.at[span], out_ref.at[index, span], sems.at[part])


def own_frames(
    a0_ref, a1_ref, first_ref, w1_any, w2_any, gain2_any, frames_any,
    p1_ref, wt1_ref, wt2_ref, m_ref, g2_ref, x0_ref,
    gain2_ref, frames_ref, x1_ref, w1_ref, w2_ref, sems,
):
    small = [
        pltpu.make_async_copy(frames_any, frames_ref, sems.at[0]),
        pltpu.make_async_copy(gain2_any, gain2_ref, sems.at[1]),
    ]
    others = pltpu.make_async_copy(w1_any.at[pl.ds(DEPTH, 2 * DEPTH)], w1_ref, sems.at[2])
    load = pltpu.make_async_copy(w2_any, w2_ref, sems.at[3])
    for copy in small + [others, load]:
        copy.start()
    for step in turn_pieces(first_ref, wt1_ref, (0,)):
        step()
    clear_edges(x1_ref)
    clear_edges(x0_ref)
    put(x1_ref, a1_ref, 0)
    put(x1_ref, a1_ref, 1)
    turn1 = turn_pieces(w1_ref, wt1_ref, (1, 2), 1)
    share = C // ROWS
    for row in range(ROWS):
        d = product(wt1_ref, 0, 1, x1_ref, row)
        put(x1_ref, a1_ref, row + 2)
        put(x0_ref, a0_ref, row)
        if row == 2:
            others.wait()
            for copy in small:
                copy.wait()
            masks = tap_masks(frames_ref)
            for i in range(8):
                m_ref[i : i + 1, :] = jnp.full((1, COLS), masks[i % 4], F32)
        if row >= 2:
            for step in turn1[(row - 2) * len(turn1) // 6 : (row - 1) * len(turn1) // 6]:
                step()
        p1_ref[row] = d
    load.wait()
    turn2 = turn_pieces(w2_ref, wt2_ref, (0, 1, 2))
    for row in range(ROWS):
        d = product(wt1_ref, 1, 2, x0_ref, row)
        for c in range(row * share, (row + 1) * share):
            g2_ref[c : c + 1, :] = jnp.full((1, COLS), gain2_ref[c], F32)
        for step in turn2[row * len(turn2) // ROWS : (row + 1) * len(turn2) // ROWS]:
            step()
        p1_ref[row] += mask(m_ref, 2) * d


def halo_first(far_ref, near_ref, o1_ref, wt_ref, g_ref, m_ref, s_ref, x_ref):
    clear_edges(x_ref)
    put_either(x_ref, far_ref, near_ref, 0)
    put_either(x_ref, far_ref, near_ref, 1)
    for row in range(ROWS):
        d = product(wt_ref, 2, 3, x_ref, row)
        put_either(x_ref, far_ref, near_ref, row + 2)
        s_ref[row] = second_activation(o1_ref[row] + mask(m_ref, 3) * d, g_ref)


def halo_middle(x0_ref, x_ref, wt1_ref, m_ref, s1_ref, wt2_ref, p_ref, q_ref, x1_ref):
    clear_edges(x1_ref)
    for row in range(ROWS):
        d = mask(m_ref, 0) * product(wt1_ref, 1, 2, x_ref, row)
        put(x1_ref, s1_ref, row)
        p_ref[row] = d + product(wt1_ref, 0, 1, x0_ref, row)
    for row in range(ROWS):
        q_ref[row] = product(wt2_ref, 0, 1, x1_ref, row)


def halo_second(h_ref, p_ref, wt_ref, g_ref, m_ref, s_ref, x_ref):
    clear_edges(x_ref)
    put(x_ref, h_ref, 0)
    put(x_ref, h_ref, 1)
    for row in range(ROWS):
        d = product(wt_ref, 2, 3, x_ref, row)
        put(x_ref, h_ref, row + 2)
        s_ref[row] = second_activation(p_ref[row] + mask(m_ref, 1) * d, g_ref)


def local_second(s0_ref, p_ref, wt_ref, m_ref, o0_ref, o1_ref, x_ref):
    clear_edges(x_ref)
    put(x_ref, s0_ref, 0)
    put(x_ref, s0_ref, 1)
    for row in range(ROWS):
        d = product(wt_ref, 0, 2, x_ref, row)
        put(x_ref, s0_ref, row + 2)
        o0_ref[row] = d[:C]
        o1_ref[row] = p_ref[row] + mask(m_ref, 2) * d[C:]


def last_frame(h_ref, o0_ref, o1_ref, wt_ref, m_ref, p_ref, t_ref, x_ref):
    clear_edges(x_ref)
    put(x_ref, h_ref, 0)
    put(x_ref, h_ref, 1)
    for row in range(ROWS):
        d = product(wt_ref, 1, 3, x_ref, row)
        put(x_ref, h_ref, row + 2)
        p_ref[row] = o0_ref[row] + mask(m_ref, 0) * d[:C]
        put_transposed(t_ref, row, o1_ref[row] + mask(m_ref, 3) * d[C:])


def other_frame(
    h_ref, p_ref, wt_ref, m_ref, t1_ref, f_ref, out_ref, t_ref, x_ref, buf0_ref, buf1_ref, sems0, sems1
):
    clear_edges(x_ref)
    put(x_ref, h_ref, 0)
    put(x_ref, h_ref, 1)
    share = C // ROWS
    for row in range(ROWS):
        d = product(wt_ref, 2, 3, x_ref, row)
        put(x_ref, h_ref, row + 2)
        for c in range(row * share, (row + 1) * share):
            finish(t1_ref, f_ref, 1, c, buf1_ref)
        put_transposed(t_ref, row, p_ref[row] + mask(m_ref, 1) * d)
        if (row + 1) % (ROWS // PARTS) == 0:
            out_copy(buf1_ref, out_ref, 1, row // (ROWS // PARTS), sems1).start()
    for part in range(PARTS):

        def step(b, _):
            for j in range(16):
                finish(t_ref, f_ref, 0, part * (C // PARTS) + b * 16 + j, buf0_ref)
            return 0

        lax.fori_loop(0, C // PARTS // 16, step, 0)
        out_copy(buf0_ref, out_ref, 0, part, sems0).start()
    for part in range(PARTS):
        out_copy(buf1_ref, out_ref, 1, part, sems1).wait()
        out_copy(buf0_ref, out_ref, 0, part, sems0).wait()


VM = pl.BlockSpec(memory_space=pltpu.VMEM)
ANY = pl.BlockSpec(memory_space=pl.ANY)
HBM = pl.BlockSpec(memory_space=pltpu.HBM)
NATURAL = pltpu.VMEM((2, C * ROWS, HALF), F32)
RAW = pltpu.VMEM((C, ROWS, COLS), BF16)
SLABS = pltpu.VMEM(((ROWS + 2) * SLAB, COLS), BF16)
FRAME = pltpu.VMEM((C, ROWS, COLS), BF16)
GAIN = pltpu.SMEM((C,), F32)
SEMS = pltpu.SemaphoreType.DMA((PARTS,))
A_SUM = jax.ShapeDtypeStruct((ROWS, C, COLS), F32)
A_ACT = jax.ShapeDtypeStruct((ROWS, C, COLS), BF16)
A_FIRST = jax.ShapeDtypeStruct((DEPTH, C), BF16)
A_RAW = jax.ShapeDtypeStruct((C, ROWS, COLS), BF16)
A_SLABS = jax.ShapeDtypeStruct(((ROWS + 2) * SLAB, COLS), BF16)
A_NATURAL = jax.ShapeDtypeStruct((2, C * ROWS, HALF), F32)
A_TURNED = jax.ShapeDtypeStruct((TAPS * C, DEPTH), BF16)
A_MASKS = jax.ShapeDtypeStruct((8, COLS), F32)
A_GAINS = jax.ShapeDtypeStruct((C, COLS), F32)
A_HALF_GAINS = jax.ShapeDtypeStruct((C, HALF), F32)


def stay(value):
    return pltpu.with_memory_space_constraint(value, pltpu.HBM)


def call(kernel, in_specs, out_shape, scratch=(), out_specs=None, aliases=None):
    return pl.pallas_call(
        kernel,
        in_specs=in_specs,
        out_specs=out_specs or jax.tree.map(lambda _: VM, out_shape),
        out_shape=out_shape,
        scratch_shapes=scratch,
        input_output_aliases=aliases or {},
        compiler_params=pltpu.CompilerParams(vmem_limit_bytes=VMEM_LIMIT),
        cost_estimate=pl.CostEstimate(flops=3 * 10**10, bytes_accessed=10**7, transcendentals=0),
        name=kernel.__name__,
    )


def per_device(features, video_frames, gain_first, conv_first, gain_second, conv_second):
    w1 = conv_first.reshape(TAPS * DEPTH, C)
    w2 = conv_second.reshape(TAPS * DEPTH, C)

    a1, raw0, first, g1 = call(
        first_sent, [HBM] * 3, [A_ACT, A_RAW, A_FIRST, A_HALF_GAINS],
        [RAW, GAIN, NATURAL, pltpu.SemaphoreType.DMA((6,)), pltpu.SemaphoreType.DMA((4,))],
    )(stay(features), stay(w1), stay(gain_first))
    a_far = to_next_pair(a1)
    first, a0, a1 = call(
        rest_sent, [VM] * 4 + [HBM] * 3, [A_FIRST, A_ACT, A_ACT],
        [
            GAIN, RAW, RAW, NATURAL, pltpu.SemaphoreType.DMA((2,)),
            pltpu.SemaphoreType.DMA((4,)), pltpu.SemaphoreType.DMA((4,)),
        ],
        aliases={3: 0},
    )(a1, raw0, g1, first, stay(features), stay(w1), stay(gain_first))
    a_earlier = shifted(a0)
    a_near = within_pair(a1)
    p1, wt1, wt2, m, g2, x0 = call(
        own_frames, [VM] * 3 + [HBM] * 4, [A_SUM, A_TURNED, A_TURNED, A_MASKS, A_GAINS, A_SLABS],
        [
            GAIN, pltpu.SMEM(video_frames.shape, jnp.int32), SLABS,
            pltpu.VMEM((2 * DEPTH, C), BF16), pltpu.VMEM((TAPS * DEPTH, C), BF16),
            pltpu.SemaphoreType.DMA((4,)),
        ],
    )(a0, a1, first, stay(w1), stay(w2), stay(gain_second), stay(video_frames))
    s1, x = call(halo_first, [VM] * 6, [A_ACT, A_SLABS])(a_far, a_near, p1, wt1, g2, m)
    s_before = shifted(s1)
    part, q = call(halo_middle, [VM] * 6, [A_SUM, A_SUM], [SLABS])(x0, x, wt1, m, s1, wt2)
    s0 = call(halo_second, [VM] * 5, A_ACT, [SLABS])(a_earlier, part, wt1, g2, m)
    s_earlier = shifted(s0)
    q0, q1 = call(local_second, [VM] * 4, [A_SUM, A_SUM], [SLABS])(s0, q, wt2, m)
    part2, t1 = call(last_frame, [VM] * 5, [A_SUM, A_NATURAL], [SLABS])(s_before, q0, q1, wt2, m)
    return call(
        other_frame, [VM] * 6, jax.ShapeDtypeStruct(features.shape, BF16),
        [NATURAL, SLABS, FRAME, FRAME, SEMS, SEMS], out_specs=ANY,
    )(s_earlier, part2, wt2, m, t1, features)


def solution(mesh):
    in_specs = (P(("group", "tm"), None, None, None), P("group"), P(), P(), P(), P())
    out_specs = P(("group", "tm"), None, None, None)
    return jax.shard_map(
        per_device, mesh=mesh, in_specs=in_specs, out_specs=out_specs, check_vma=False
    )
```

```python
import jax
import jax.numpy as jnp
from jax import lax
from jax.experimental import pallas as pl
from jax.experimental.pallas import tpu as pltpu
from jax.sharding import PartitionSpec as P

C = 192
ROWS = 8
COLS = 256
HALF = 128
TAPS = 3
SLAB = 3 * C
DEPTH = 9 * C
PIECE = 384
PARTS = 4
EPS = 1e-06
VMEM_LIMIT = 18 * 1024 * 1024
F32 = jnp.float32
BF16 = jnp.bfloat16


def shifted(value):
    return lax.ppermute(value, "tm", [(i, i + 1) for i in range(lax.axis_size("tm") - 1)])


def to_next_pair(value):
    return lax.ppermute(value, "tm", [(i, i + 1) for i in range(1, lax.axis_size("tm") - 1, 2)])


def within_pair(value):
    return lax.ppermute(value, "tm", [(i, i + 1) for i in range(0, lax.axis_size("tm"), 2)])


def tap_masks(frames_ref):
    first = 2 * lax.axis_index("tm")

    def step(v, carry):
        begin, start0, start1 = carry
        start0 = jnp.where(begin <= first, begin, start0)
        start1 = jnp.where(begin <= first + 1, begin, start1)
        return begin + frames_ref[v], start0, start1

    zero = jnp.int32(0)
    _, start0, start1 = lax.fori_loop(0, frames_ref.shape[0], step, (zero, zero, zero))
    return tuple(
        jnp.where(test, 1.0, 0.0).astype(F32)
        for test in (
            first - 1 >= start0,
            first - 2 >= start0,
            first >= start1,
            first - 1 >= start1,
        )
    )


def mask(m_ref, i):
    return m_ref[i : i + 1, :]


def turn_pieces(w_ref, wt_ref, taps):
    def turn(k, lo, hi):
        base = k * DEPTH
        wt_ref[k * C : (k + 1) * C, lo:hi] = w_ref[base + lo : base + hi, :].T

    return [
        (lambda k=k, lo=lo: turn(k, lo, min(lo + PIECE, DEPTH)))
        for k in taps
        for lo in range(0, DEPTH, PIECE)
    ]


def put_row(x_ref, row, values):
    base = (row + 1) * SLAB
    cols = lax.broadcasted_iota(jnp.int32, (C, COLS), 1)
    left = jnp.where(cols == 0, 0.0, pltpu.roll(values, 1, 1))
    right = jnp.where(cols == COLS - 1, 0.0, pltpu.roll(values, COLS - 1, 1))
    x_ref[base : base + C, :] = left.astype(BF16)
    x_ref[base + C : base + 2 * C, :] = values.astype(BF16)
    x_ref[base + 2 * C : base + 3 * C, :] = right.astype(BF16)


def clear_edges(x_ref):
    zeros = jnp.zeros((SLAB, COLS), BF16)
    x_ref[0:SLAB, :] = zeros
    x_ref[(ROWS + 1) * SLAB : (ROWS + 2) * SLAB, :] = zeros


def put(x_ref, a_ref, row):
    if row < ROWS:
        put_row(x_ref, row, a_ref[row].astype(F32))


def put_either(x_ref, far_ref, near_ref, row):
    if row < ROWS:
        put_row(x_ref, row, far_ref[row].astype(F32) + near_ref[row].astype(F32))


def product(wt_ref, lo, hi, x_ref, row):
    return jnp.dot(
        wt_ref[lo * C : hi * C, :],
        x_ref[row * SLAB : row * SLAB + DEPTH, :],
        preferred_element_type=F32,
    )


def sends_far():
    return lax.rem(lax.axis_index("tm"), 2) == 1


def inverse_rms(raw_ref, h):
    cols = slice(h * HALF, (h + 1) * HALF)

    def squares(b, total):
        v = raw_ref[pl.ds(b * 16, 16), :, cols].astype(F32)
        return total + jnp.sum(v * v, axis=0)

    total = lax.fori_loop(0, C // 16, squares, jnp.zeros((ROWS, HALF), F32))
    return lax.rsqrt(total * (1.0 / C) + EPS)


def activate(raw_ref, h, c, inverse, gain, t_ref):
    u = raw_ref[c, :, h * HALF : (h + 1) * HALF].astype(F32) * inverse * gain
    t_ref[h, c * ROWS : (c + 1) * ROWS, :] = u * jax.nn.sigmoid(u)


def row_of(t_ref, h, row):
    return t_ref[h, pl.ds(row, C, stride=ROWS), :]


def to_rows(t_ref, h, a_ref):
    for row in range(ROWS):
        a_ref[row, :, h * HALF : (h + 1) * HALF] = row_of(t_ref, h, row).astype(BF16)


def frame_copies(f_ref, index, raw_ref, sems):
    return [
        [
            pltpu.make_async_copy(
                f_ref.at[index, pl.ds(q * C // 2, C // 2), :, pl.ds(h * HALF, HALF)],
                raw_ref.at[pl.ds(q * C // 2, C // 2), :, pl.ds(h * HALF, HALF)],
                sems.at[2 * h + q],
            )
            for q in range(2)
        ]
        for h in range(2)
    ]


def taps_copy(w_any, w_ref, lo, hi, sem):
    span = pl.ds(lo * DEPTH, (hi - lo) * DEPTH)
    return pltpu.make_async_copy(w_any.at[span], w_ref.at[span], sem)


def flat(copies):
    return copies[0] + copies[1]


def activate_frame(raw_ref, gain, t_ref, a_ref, before=None, extra=None):
    for h in range(2):
        if before:
            before(h)
        inverse = inverse_rms(raw_ref, h)
        for c in range(C):
            activate(raw_ref, h, c, inverse, gain(c), t_ref)
            if extra and h == 0:
                extra(c)
        to_rows(t_ref, h, a_ref)


def waits(copies):
    def wait(h):
        for copy in copies[h]:
            copy.wait()

    return wait


def first_sent(
    f_ref, w1_any, gain_any, a_ref, raw0_ref, w_ref, g1_ref, raw1_ref, gain_ref, t_ref, sems, sems0
):
    @pl.when(sends_far())
    def _():
        copies = frame_copies(f_ref, 1, raw1_ref, sems)
        gains = pltpu.make_async_copy(gain_any, gain_ref, sems.at[4])
        later = [taps_copy(w1_any, w_ref, 0, 1, sems.at[5])] + flat(frame_copies(f_ref, 0, raw0_ref, sems0))
        for copy in copies[0] + [gains] + copies[1] + later:
            copy.start()

        def before(h):
            waits(copies)(h)
            if h == 0:
                gains.wait()

        def spread(c):
            g1_ref[c : c + 1, :] = jnp.full((1, HALF), gain_ref[c], F32)

        activate_frame(raw1_ref, lambda c: gain_ref[c], t_ref, a_ref, before, spread)
        for copy in later:
            copy.wait()


def rest_sent(
    a_ref, raw0_ref, g1_ref, _, f_ref, w1_any, gain_any,
    w_ref, a0_ref, a1_ref, gain_ref, raw_ref, last_ref, t_ref, sems, sems0, sems1,
):
    far = sends_far()

    @pl.when(far)
    def _():
        others = taps_copy(w1_any, w_ref, 1, TAPS, sems.at[0])
        others.start()
        a1_ref[...] = a_ref[...]
        activate_frame(raw0_ref, lambda c: g1_ref[c : c + 1, :], t_ref, a0_ref)
        others.wait()

    @pl.when(jnp.logical_not(far))
    def _():
        gains = pltpu.make_async_copy(gain_any, gain_ref, sems.at[0])
        first = taps_copy(w1_any, w_ref, 0, TAPS, sems.at[1])
        last = frame_copies(f_ref, 1, last_ref, sems1)
        other = frame_copies(f_ref, 0, raw_ref, sems0)
        for copy in last[0] + [gains] + last[1] + flat(other) + [first]:
            copy.start()
        gains.wait()
        activate_frame(last_ref, lambda c: gain_ref[c], t_ref, a1_ref, waits(last))
        activate_frame(raw_ref, lambda c: gain_ref[c], t_ref, a0_ref, waits(other))
        first.wait()


def second_activation(values, g_ref):
    mean_square = jnp.sum(values * values, axis=0, keepdims=True) * (1.0 / C)
    u = values * lax.rsqrt(mean_square + EPS) * g_ref[...]
    return (u * jax.nn.sigmoid(u)).astype(BF16)


def put_transposed(t_ref, row, values):
    t_ref[0, pl.ds(row, C, stride=ROWS), :] = values[:, :HALF]
    t_ref[1, pl.ds(row, C, stride=ROWS), :] = values[:, HALF:]


def finish(t_ref, f_ref, index, c, buf_ref):
    at = c * ROWS if isinstance(c, int) else pl.multiple_of(c * ROWS, ROWS)
    v = jnp.concatenate([t_ref[h, pl.ds(at, ROWS), :] for h in range(2)], axis=1)
    buf_ref[c] = (f_ref[index, c].astype(F32) + v).astype(BF16)


def out_copy(buf_ref, out_ref, index, part, sems):
    span = pl.ds(part * (C // PARTS), C // PARTS)
    return pltpu.make_async_copy(buf_ref.at[span], out_ref.at[index, span], sems.at[part])


def own_frames(
    a0_ref, a1_ref, w1_ref, w2_any, gain2_any, frames_any,
    p1_ref, wt1_ref, wt2_ref, m_ref, g2_ref, x0_ref,
    gain2_ref, frames_ref, x1_ref, w2_ref, sems,
):
    small = [
        pltpu.make_async_copy(frames_any, frames_ref, sems.at[0]),
        pltpu.make_async_copy(gain2_any, gain2_ref, sems.at[1]),
    ]
    load = pltpu.make_async_copy(w2_any, w2_ref, sems.at[2])
    for copy in small + [load]:
        copy.start()
    for step in turn_pieces(w1_ref, wt1_ref, (0,)):
        step()
    clear_edges(x1_ref)
    clear_edges(x0_ref)
    put(x1_ref, a1_ref, 0)
    put(x1_ref, a1_ref, 1)
    turn1 = turn_pieces(w1_ref, wt1_ref, (1, 2))
    share = C // ROWS
    for row in range(ROWS):
        d = product(wt1_ref, 0, 1, x1_ref, row)
        put(x1_ref, a1_ref, row + 2)
        put(x0_ref, a0_ref, row)
        if row == 2:
            for copy in small:
                copy.wait()
            masks = tap_masks(frames_ref)
            for i in range(8):
                m_ref[i : i + 1, :] = jnp.full((1, COLS), masks[i % 4], F32)
        for step in turn1[row * len(turn1) // ROWS : (row + 1) * len(turn1) // ROWS]:
            step()
        p1_ref[row] = d
    load.wait()
    turn2 = turn_pieces(w2_ref, wt2_ref, (0, 1, 2))
    for row in range(ROWS):
        d = product(wt1_ref, 1, 2, x0_ref, row)
        for c in range(row * share, (row + 1) * share):
            g2_ref[c : c + 1, :] = jnp.full((1, COLS), gain2_ref[c], F32)
        for step in turn2[row * len(turn2) // ROWS : (row + 1) * len(turn2) // ROWS]:
            step()
        p1_ref[row] += mask(m_ref, 2) * d


def halo_first(far_ref, near_ref, o1_ref, wt_ref, g_ref, m_ref, s_ref, x_ref):
    clear_edges(x_ref)
    put_either(x_ref, far_ref, near_ref, 0)
    put_either(x_ref, far_ref, near_ref, 1)
    for row in range(ROWS):
        d = product(wt_ref, 2, 3, x_ref, row)
        put_either(x_ref, far_ref, near_ref, row + 2)
        s_ref[row] = second_activation(o1_ref[row] + mask(m_ref, 3) * d, g_ref)


def halo_middle(x0_ref, x_ref, wt_ref, m_ref, p_ref):
    for row in range(ROWS):
        d = mask(m_ref, 0) * product(wt_ref, 1, 2, x_ref, row)
        p_ref[row] = d + product(wt_ref, 0, 1, x0_ref, row)


def halo_second(h_ref, p_ref, wt1_ref, wt2_ref, g_ref, m_ref, sent_ref, x0_ref, x_ref):
    clear_edges(x_ref)
    clear_edges(x0_ref)
    put(x_ref, h_ref, 0)
    put(x_ref, h_ref, 1)
    for row in range(ROWS + 1):
        if row < ROWS:
            d = product(wt1_ref, 2, 3, x_ref, row)
            put(x_ref, h_ref, row + 2)
            act = second_activation(p_ref[row] + mask(m_ref, 1) * d, g_ref)
            put_row(x0_ref, row, act.astype(F32))
        if row > 0:
            sent_ref[row - 1] = product(wt2_ref, 2, 3, x0_ref, row - 1).astype(BF16)


def local_second(x0_ref, s1_ref, wt_ref, m_ref, o0_ref, o1_ref, x1_ref):
    clear_edges(x1_ref)
    for row in range(ROWS):
        d = product(wt_ref, 0, 2, x0_ref, row)
        put(x1_ref, s1_ref, row)
        o0_ref[row] = d[:C]
        o1_ref[row] = mask(m_ref, 2) * d[C:]
    for row in range(ROWS):
        o1_ref[row] += product(wt_ref, 0, 1, x1_ref, row)


def finish(t_ref, f_ref, index, c, buf_ref):
    v = jnp.concatenate([t_ref[h, c * ROWS : (c + 1) * ROWS, :] for h in range(2)], axis=1)
    buf_ref[c] = (f_ref[index, c].astype(F32) + v).astype(BF16)


def write_frame(t_ref, f_ref, index, buf_ref, out_ref, sems):
    step = C // PARTS
    copies = []
    for part in range(PARTS):
        for c in range(part * step, (part + 1) * step):
            finish(t_ref, f_ref, index, c, buf_ref)
        span = pl.ds(part * step, step)
        copies.append(pltpu.make_async_copy(buf_ref.at[span], out_ref.at[index, span], sems.at[part]))
        copies[-1].start()
    for copy in copies:
        copy.wait()


def last_frame(h_ref, o0_ref, o1_ref, wt_ref, m_ref, f_ref, p_ref, out_ref, t_ref, x_ref, buf_ref, sems):
    clear_edges(x_ref)
    put(x_ref, h_ref, 0)
    put(x_ref, h_ref, 1)
    for row in range(ROWS):
        d = product(wt_ref, 1, 3, x_ref, row)
        put(x_ref, h_ref, row + 2)
        p_ref[row] = o0_ref[row] + mask(m_ref, 0) * d[:C]
        put_transposed(t_ref, row, o1_ref[row] + mask(m_ref, 3) * d[C:])
    write_frame(t_ref, f_ref, 1, buf_ref, out_ref, sems)


def first_frame(d_ref, p_ref, m_ref, f_ref, _, out_ref, t_ref, buf_ref, sems):
    for row in range(ROWS):
        put_transposed(t_ref, row, p_ref[row] + mask(m_ref, 1) * d_ref[row].astype(F32))
    write_frame(t_ref, f_ref, 0, buf_ref, out_ref, sems)


VM = pl.BlockSpec(memory_space=pltpu.VMEM)
ANY = pl.BlockSpec(memory_space=pl.ANY)
HBM = pl.BlockSpec(memory_space=pltpu.HBM)
NATURAL = pltpu.VMEM((2, C * ROWS, HALF), F32)
RAW = pltpu.VMEM((C, ROWS, COLS), BF16)
SLABS = pltpu.VMEM(((ROWS + 2) * SLAB, COLS), BF16)
FRAME = pltpu.VMEM((C, ROWS, COLS), BF16)
GAIN = pltpu.SMEM((C,), F32)
SEMS = pltpu.SemaphoreType.DMA((PARTS,))
A_SUM = jax.ShapeDtypeStruct((ROWS, C, COLS), F32)
A_ACT = jax.ShapeDtypeStruct((ROWS, C, COLS), BF16)
A_WEIGHTS = jax.ShapeDtypeStruct((TAPS * DEPTH, C), BF16)
A_RAW = jax.ShapeDtypeStruct((C, ROWS, COLS), BF16)
A_SLABS = jax.ShapeDtypeStruct(((ROWS + 2) * SLAB, COLS), BF16)
A_NATURAL = jax.ShapeDtypeStruct((2, C * ROWS, HALF), F32)
A_TURNED = jax.ShapeDtypeStruct((TAPS * C, DEPTH), BF16)
A_MASKS = jax.ShapeDtypeStruct((8, COLS), F32)
A_GAINS = jax.ShapeDtypeStruct((C, COLS), F32)
A_HALF_GAINS = jax.ShapeDtypeStruct((C, HALF), F32)


def stay(value):
    return pltpu.with_memory_space_constraint(value, pltpu.HBM)


def call(kernel, in_specs, out_shape, scratch=(), out_specs=None, aliases=None, flops=3 * 10**10):
    return pl.pallas_call(
        kernel,
        in_specs=in_specs,
        out_specs=out_specs or jax.tree.map(lambda _: VM, out_shape),
        out_shape=out_shape,
        scratch_shapes=scratch,
        input_output_aliases=aliases or {},
        compiler_params=pltpu.CompilerParams(vmem_limit_bytes=VMEM_LIMIT),
        cost_estimate=pl.CostEstimate(flops=flops, bytes_accessed=10**7, transcendentals=0),
        name=kernel.__name__,
    )


def per_device(features, video_frames, gain_first, conv_first, gain_second, conv_second):
    w1 = conv_first.reshape(TAPS * DEPTH, C)
    w2 = conv_second.reshape(TAPS * DEPTH, C)

    a1, raw0, held, g1 = call(
        first_sent, [HBM] * 3, [A_ACT, A_RAW, A_WEIGHTS, A_HALF_GAINS],
        [RAW, GAIN, NATURAL, pltpu.SemaphoreType.DMA((6,)), pltpu.SemaphoreType.DMA((4,))],
    )(stay(features), stay(w1), stay(gain_first))
    a_far = to_next_pair(a1)
    w1, a0, a1 = call(
        rest_sent, [VM] * 4 + [HBM] * 3, [A_WEIGHTS, A_ACT, A_ACT],
        [
            GAIN, RAW, RAW, NATURAL, pltpu.SemaphoreType.DMA((2,)),
            pltpu.SemaphoreType.DMA((4,)), pltpu.SemaphoreType.DMA((4,)),
        ],
        aliases={3: 0},
    )(a1, raw0, g1, held, stay(features), stay(w1), stay(gain_first))
    a_earlier = shifted(a0)
    a_near = within_pair(a1)
    p1, wt1, wt2, m, g2, x0 = call(
        own_frames, [VM] * 3 + [HBM] * 3, [A_SUM, A_TURNED, A_TURNED, A_MASKS, A_GAINS, A_SLABS],
        [
            GAIN, pltpu.SMEM(video_frames.shape, jnp.int32), SLABS,
            pltpu.VMEM((TAPS * DEPTH, C), BF16), pltpu.SemaphoreType.DMA((3,)),
        ],
    )(a0, a1, w1, stay(w2), stay(gain_second), stay(video_frames))
    s1, x = call(halo_first, [VM] * 6, [A_ACT, A_SLABS])(a_far, a_near, p1, wt1, g2, m)
    s_before = shifted(s1)
    part = call(halo_middle, [VM] * 4, A_SUM)(x0, x, wt1, m)
    sent, x0 = call(halo_second, [VM] * 6, [A_ACT, A_SLABS], [SLABS])(a_earlier, part, wt1, wt2, g2, m)
    d_earlier = shifted(sent)
    q0, q1 = call(local_second, [VM] * 4, [A_SUM, A_SUM], [SLABS], flops=10**10)(x0, s1, wt2, m)
    whole = jax.ShapeDtypeStruct(features.shape, BF16)
    part, out = call(
        last_frame, [VM] * 6, [A_SUM, whole], [NATURAL, SLABS, FRAME, SEMS], [VM, ANY], flops=10**10,
    )(s_before, q0, q1, wt2, m, features)
    return call(
        first_frame, [VM] * 4 + [ANY], whole, [NATURAL, FRAME, SEMS], ANY, {4: 0}
    )(d_earlier, part, m, features, out)


def solution(mesh):
    in_specs = (P(("group", "tm"), None, None, None), P("group"), P(), P(), P(), P())
    out_specs = P(("group", "tm"), None, None, None)
    return jax.shard_map(
        per_device, mesh=mesh, in_specs=in_specs, out_specs=out_specs, check_vma=False
    )
```

```python
import jax
import jax.numpy as jnp
from jax import lax
from jax.experimental import pallas as pl
from jax.experimental.pallas import tpu as pltpu
from jax.sharding import PartitionSpec as P

C = 192
ROWS = 8
COLS = 256
HALF = 128
TAPS = 3
SLAB = 3 * C
DEPTH = 9 * C
PIECE = 384
PARTS = 4
EPS = 1e-06
VMEM_LIMIT = 18 * 1024 * 1024
F32 = jnp.float32
BF16 = jnp.bfloat16


def shifted(value):
    return lax.ppermute(value, "tm", [(i, i + 1) for i in range(lax.axis_size("tm") - 1)])


def to_next_pair(value):
    return lax.ppermute(value, "tm", [(i, i + 1) for i in range(1, lax.axis_size("tm") - 1, 2)])


def within_pair(value):
    return lax.ppermute(value, "tm", [(i, i + 1) for i in range(0, lax.axis_size("tm"), 2)])


def tap_masks(frames_ref):
    first = 2 * lax.axis_index("tm")

    def step(v, carry):
        begin, start0, start1 = carry
        start0 = jnp.where(begin <= first, begin, start0)
        start1 = jnp.where(begin <= first + 1, begin, start1)
        return begin + frames_ref[v], start0, start1

    zero = jnp.int32(0)
    _, start0, start1 = lax.fori_loop(0, frames_ref.shape[0], step, (zero, zero, zero))
    return tuple(
        jnp.where(test, 1.0, 0.0).astype(F32)
        for test in (
            first - 1 >= start0,
            first - 2 >= start0,
            first >= start1,
            first - 1 >= start1,
        )
    )


def mask(m_ref, i):
    return m_ref[i : i + 1, :]


def turn_pieces(w_ref, wt_ref, taps):
    def turn(k, lo, hi):
        base = k * DEPTH
        wt_ref[k * C : (k + 1) * C, lo:hi] = w_ref[base + lo : base + hi, :].T

    return [
        (lambda k=k, lo=lo: turn(k, lo, min(lo + PIECE, DEPTH)))
        for k in taps
        for lo in range(0, DEPTH, PIECE)
    ]


def put_row(x_ref, row, values):
    base = (row + 1) * SLAB
    cols = lax.broadcasted_iota(jnp.int32, (C, COLS), 1)
    left = jnp.where(cols == 0, 0.0, pltpu.roll(values, 1, 1))
    right = jnp.where(cols == COLS - 1, 0.0, pltpu.roll(values, COLS - 1, 1))
    x_ref[base : base + C, :] = left.astype(BF16)
    x_ref[base + C : base + 2 * C, :] = values.astype(BF16)
    x_ref[base + 2 * C : base + 3 * C, :] = right.astype(BF16)


def clear_edges(x_ref):
    zeros = jnp.zeros((SLAB, COLS), BF16)
    x_ref[0:SLAB, :] = zeros
    x_ref[(ROWS + 1) * SLAB : (ROWS + 2) * SLAB, :] = zeros


def put(x_ref, a_ref, row):
    if row < ROWS:
        put_row(x_ref, row, a_ref[row].astype(F32))


def put_either(x_ref, far_ref, near_ref, row):
    if row < ROWS:
        put_row(x_ref, row, far_ref[row].astype(F32) + near_ref[row].astype(F32))


def product(wt_ref, lo, hi, x_ref, row):
    return jnp.dot(
        wt_ref[lo * C : hi * C, :],
        x_ref[row * SLAB : row * SLAB + DEPTH, :],
        preferred_element_type=F32,
    )


def sends_far():
    return lax.rem(lax.axis_index("tm"), 2) == 1


def inverse_rms(raw_ref, h):
    cols = slice(h * HALF, (h + 1) * HALF)

    def squares(b, total):
        v = raw_ref[pl.ds(b * 16, 16), :, cols].astype(F32)
        return total + jnp.sum(v * v, axis=0)

    total = lax.fori_loop(0, C // 16, squares, jnp.zeros((ROWS, HALF), F32))
    return lax.rsqrt(total * (1.0 / C) + EPS)


def activate(raw_ref, h, c, inverse, gain, t_ref):
    u = raw_ref[c, :, h * HALF : (h + 1) * HALF].astype(F32) * inverse * gain
    t_ref[h, c * ROWS : (c + 1) * ROWS, :] = u * jax.nn.sigmoid(u)


def row_of(t_ref, h, row):
    return t_ref[h, pl.ds(row, C, stride=ROWS), :]


def to_rows(t_ref, h, a_ref):
    for row in range(ROWS):
        a_ref[row, :, h * HALF : (h + 1) * HALF] = row_of(t_ref, h, row).astype(BF16)


def frame_copies(f_ref, index, raw_ref, sems):
    return [
        [
            pltpu.make_async_copy(
                f_ref.at[index, pl.ds(q * C // 2, C // 2), :, pl.ds(h * HALF, HALF)],
                raw_ref.at[pl.ds(q * C // 2, C // 2), :, pl.ds(h * HALF, HALF)],
                sems.at[2 * h + q],
            )
            for q in range(2)
        ]
        for h in range(2)
    ]


def taps_copy(w_any, w_ref, lo, hi, sem):
    span = pl.ds(lo * DEPTH, (hi - lo) * DEPTH)
    return pltpu.make_async_copy(w_any.at[span], w_ref.at[span], sem)


def flat(copies):
    return copies[0] + copies[1]


def activate_frame(raw_ref, gain, t_ref, a_ref, before=None, extra=None):
    for h in range(2):
        if before:
            before(h)
        inverse = inverse_rms(raw_ref, h)
        for c in range(C):
            activate(raw_ref, h, c, inverse, gain(c), t_ref)
            if extra and h == 0:
                extra(c)
        to_rows(t_ref, h, a_ref)


def waits(copies):
    def wait(h):
        for copy in copies[h]:
            copy.wait()

    return wait


def first_sent(
    f_ref, w1_any, gain_any, a_ref, raw0_ref, w_ref, g1_ref, raw1_ref, gain_ref, t_ref, sems, sems0
):
    @pl.when(sends_far())
    def _():
        copies = frame_copies(f_ref, 1, raw1_ref, sems)
        gains = pltpu.make_async_copy(gain_any, gain_ref, sems.at[4])
        later = [taps_copy(w1_any, w_ref, 0, 1, sems.at[5])] + flat(frame_copies(f_ref, 0, raw0_ref, sems0))
        for copy in copies[0] + [gains] + copies[1] + later:
            copy.start()

        def before(h):
            waits(copies)(h)
            if h == 0:
                gains.wait()

        def spread(c):
            g1_ref[c : c + 1, :] = jnp.full((1, HALF), gain_ref[c], F32)

        activate_frame(raw1_ref, lambda c: gain_ref[c], t_ref, a_ref, before, spread)
        for copy in later:
            copy.wait()


def rest_sent(
    a_ref, raw0_ref, g1_ref, _, f_ref, w1_any, gain_any,
    w_ref, a0_ref, a1_ref, gain_ref, raw_ref, last_ref, t_ref, sems, sems0, sems1,
):
    far = sends_far()

    @pl.when(far)
    def _():
        others = taps_copy(w1_any, w_ref, 1, TAPS, sems.at[0])
        others.start()
        a1_ref[...] = a_ref[...]
        activate_frame(raw0_ref, lambda c: g1_ref[c : c + 1, :], t_ref, a0_ref)
        others.wait()

    @pl.when(jnp.logical_not(far))
    def _():
        gains = pltpu.make_async_copy(gain_any, gain_ref, sems.at[0])
        first = taps_copy(w1_any, w_ref, 0, TAPS, sems.at[1])
        last = frame_copies(f_ref, 1, last_ref, sems1)
        other = frame_copies(f_ref, 0, raw_ref, sems0)
        for copy in last[0] + [gains] + last[1] + flat(other) + [first]:
            copy.start()
        gains.wait()
        activate_frame(last_ref, lambda c: gain_ref[c], t_ref, a1_ref, waits(last))
        activate_frame(raw_ref, lambda c: gain_ref[c], t_ref, a0_ref, waits(other))
        first.wait()


def second_activation(values, g_ref):
    mean_square = jnp.sum(values * values, axis=0, keepdims=True) * (1.0 / C)
    u = values * lax.rsqrt(mean_square + EPS) * g_ref[...]
    return (u * jax.nn.sigmoid(u)).astype(BF16)


def put_transposed(t_ref, row, values):
    t_ref[0, pl.ds(row, C, stride=ROWS), :] = values[:, :HALF]
    t_ref[1, pl.ds(row, C, stride=ROWS), :] = values[:, HALF:]


def own_frames(
    a0_ref, a1_ref, w1_ref, w2_any, gain2_any, frames_any,
    p1_ref, wt1_ref, wt2_ref, m_ref, g2_ref, x0_ref,
    gain2_ref, frames_ref, x1_ref, w2_ref, sems,
):
    small = [
        pltpu.make_async_copy(frames_any, frames_ref, sems.at[0]),
        pltpu.make_async_copy(gain2_any, gain2_ref, sems.at[1]),
    ]
    load = pltpu.make_async_copy(w2_any, w2_ref, sems.at[2])
    for copy in small + [load]:
        copy.start()
    for step in turn_pieces(w1_ref, wt1_ref, (0,)):
        step()
    clear_edges(x1_ref)
    clear_edges(x0_ref)
    put(x1_ref, a1_ref, 0)
    put(x1_ref, a1_ref, 1)
    turn1 = turn_pieces(w1_ref, wt1_ref, (1, 2))
    share = C // ROWS
    for row in range(ROWS):
        d = product(wt1_ref, 0, 1, x1_ref, row)
        put(x1_ref, a1_ref, row + 2)
        put(x0_ref, a0_ref, row)
        if row == 2:
            for copy in small:
                copy.wait()
            masks = tap_masks(frames_ref)
            for i in range(8):
                m_ref[i : i + 1, :] = jnp.full((1, COLS), masks[i % 4], F32)
        for step in turn1[row * len(turn1) // ROWS : (row + 1) * len(turn1) // ROWS]:
            step()
        p1_ref[row] = d
    load.wait()
    turn2 = turn_pieces(w2_ref, wt2_ref, (0, 1, 2))
    for row in range(ROWS):
        d = product(wt1_ref, 1, 2, x0_ref, row)
        for c in range(row * share, (row + 1) * share):
            g2_ref[c : c + 1, :] = jnp.full((1, COLS), gain2_ref[c], F32)
        for step in turn2[row * len(turn2) // ROWS : (row + 1) * len(turn2) // ROWS]:
            step()
        p1_ref[row] += mask(m_ref, 2) * d


def halo_first(far_ref, near_ref, o1_ref, wt_ref, g_ref, m_ref, s_ref, x_ref):
    clear_edges(x_ref)
    put_either(x_ref, far_ref, near_ref, 0)
    put_either(x_ref, far_ref, near_ref, 1)
    for row in range(ROWS):
        d = product(wt_ref, 2, 3, x_ref, row)
        put_either(x_ref, far_ref, near_ref, row + 2)
        s_ref[row] = second_activation(o1_ref[row] + mask(m_ref, 3) * d, g_ref)


def halo_middle(x0_ref, x_ref, wt_ref, m_ref, p_ref):
    for row in range(ROWS):
        d = mask(m_ref, 0) * product(wt_ref, 1, 2, x_ref, row)
        p_ref[row] = d + product(wt_ref, 0, 1, x0_ref, row)


def next_product(wt_ref, x_ref, sent_ref):
    for row in range(ROWS):
        sent_ref[row] = product(wt_ref, 2, 3, x_ref, row).astype(BF16)


def halo_second(h_ref, p_ref, wt1_ref, wt2_ref, g_ref, m_ref, sent_ref, x0_ref, x_ref):
    clear_edges(x_ref)
    clear_edges(x0_ref)
    put(x_ref, h_ref, 0)
    put(x_ref, h_ref, 1)
    for row in range(ROWS):
        d = product(wt1_ref, 2, 3, x_ref, row)
        put(x_ref, h_ref, row + 2)
        act = second_activation(p_ref[row] + mask(m_ref, 1) * d, g_ref)
        put_row(x0_ref, row, act.astype(F32))

    @pl.when(sends_far())
    def _():
        next_product(wt2_ref, x0_ref, sent_ref)


def first_part(x0_ref, wt_ref, m_ref, o0_ref, o1_ref):
    for row in range(ROWS):
        d = product(wt_ref, 0, 2, x0_ref, row)
        o0_ref[row] = d[:C]
        o1_ref[row] = mask(m_ref, 2) * d[C:]


def near_second(x0_ref, wt_ref, m_ref, o0_ref, o1_ref, sent_ref):
    @pl.when(jnp.logical_not(sends_far()))
    def _():
        next_product(wt_ref, x0_ref, sent_ref)
        first_part(x0_ref, wt_ref, m_ref, o0_ref, o1_ref)


def local_second(x0_ref, s1_ref, wt_ref, m_ref, _, __, o0_ref, o1_ref, x1_ref):
    @pl.when(sends_far())
    def _():
        first_part(x0_ref, wt_ref, m_ref, o0_ref, o1_ref)

    clear_edges(x1_ref)
    for row in range(ROWS):
        put(x1_ref, s1_ref, row)
    for row in range(ROWS):
        o1_ref[row] += product(wt_ref, 0, 1, x1_ref, row)


def finish(t_ref, f_ref, index, c, buf_ref):
    v = jnp.concatenate([t_ref[h, c * ROWS : (c + 1) * ROWS, :] for h in range(2)], axis=1)
    buf_ref[c] = (f_ref[index, c].astype(F32) + v).astype(BF16)


def write_frame(t_ref, f_ref, index, buf_ref, out_ref, sems):
    step = C // PARTS
    copies = []
    for part in range(PARTS):
        for c in range(part * step, (part + 1) * step):
            finish(t_ref, f_ref, index, c, buf_ref)
        span = pl.ds(part * step, step)
        copies.append(pltpu.make_async_copy(buf_ref.at[span], out_ref.at[index, span], sems.at[part]))
        copies[-1].start()
    for copy in copies:
        copy.wait()


def last_frame(h_ref, o0_ref, o1_ref, wt_ref, m_ref, f_ref, p_ref, out_ref, t_ref, x_ref, buf_ref, sems):
    clear_edges(x_ref)
    put(x_ref, h_ref, 0)
    put(x_ref, h_ref, 1)
    for row in range(ROWS):
        d = product(wt_ref, 1, 3, x_ref, row)
        put(x_ref, h_ref, row + 2)
        p_ref[row] = o0_ref[row] + mask(m_ref, 0) * d[:C]
        put_transposed(t_ref, row, o1_ref[row] + mask(m_ref, 3) * d[C:])
    write_frame(t_ref, f_ref, 1, buf_ref, out_ref, sems)


def first_frame(d_ref, p_ref, m_ref, f_ref, out_ref, t_ref, buf_ref, sems):
    for row in range(ROWS):
        put_transposed(t_ref, row, p_ref[row] + mask(m_ref, 1) * d_ref[row].astype(F32))
    write_frame(t_ref, f_ref, 0, buf_ref, out_ref, sems)


def from_far(d_ref, p_ref, m_ref, f_ref, _, out_ref, *scratch):
    @pl.when(jnp.logical_not(sends_far()))
    def _():
        first_frame(d_ref, p_ref, m_ref, f_ref, out_ref, *scratch)


def from_near(d_ref, p_ref, m_ref, f_ref, _, out_ref, *scratch):
    @pl.when(sends_far())
    def _():
        first_frame(d_ref, p_ref, m_ref, f_ref, out_ref, *scratch)


VM = pl.BlockSpec(memory_space=pltpu.VMEM)
ANY = pl.BlockSpec(memory_space=pl.ANY)
HBM = pl.BlockSpec(memory_space=pltpu.HBM)
NATURAL = pltpu.VMEM((2, C * ROWS, HALF), F32)
RAW = pltpu.VMEM((C, ROWS, COLS), BF16)
SLABS = pltpu.VMEM(((ROWS + 2) * SLAB, COLS), BF16)
FRAME = pltpu.VMEM((C, ROWS, COLS), BF16)
GAIN = pltpu.SMEM((C,), F32)
SEMS = pltpu.SemaphoreType.DMA((PARTS,))
A_SUM = jax.ShapeDtypeStruct((ROWS, C, COLS), F32)
A_ACT = jax.ShapeDtypeStruct((ROWS, C, COLS), BF16)
A_WEIGHTS = jax.ShapeDtypeStruct((TAPS * DEPTH, C), BF16)
A_RAW = jax.ShapeDtypeStruct((C, ROWS, COLS), BF16)
A_SLABS = jax.ShapeDtypeStruct(((ROWS + 2) * SLAB, COLS), BF16)
A_NATURAL = jax.ShapeDtypeStruct((2, C * ROWS, HALF), F32)
A_TURNED = jax.ShapeDtypeStruct((TAPS * C, DEPTH), BF16)
A_MASKS = jax.ShapeDtypeStruct((8, COLS), F32)
A_GAINS = jax.ShapeDtypeStruct((C, COLS), F32)
A_HALF_GAINS = jax.ShapeDtypeStruct((C, HALF), F32)


def stay(value):
    return pltpu.with_memory_space_constraint(value, pltpu.HBM)


def call(kernel, in_specs, out_shape, scratch=(), out_specs=None, aliases=None, flops=3 * 10**10):
    return pl.pallas_call(
        kernel,
        in_specs=in_specs,
        out_specs=out_specs or jax.tree.map(lambda _: VM, out_shape),
        out_shape=out_shape,
        scratch_shapes=scratch,
        input_output_aliases=aliases or {},
        compiler_params=pltpu.CompilerParams(vmem_limit_bytes=VMEM_LIMIT),
        cost_estimate=pl.CostEstimate(flops=flops, bytes_accessed=10**7, transcendentals=0),
        name=kernel.__name__,
    )


def per_device(features, video_frames, gain_first, conv_first, gain_second, conv_second):
    w1 = conv_first.reshape(TAPS * DEPTH, C)
    w2 = conv_second.reshape(TAPS * DEPTH, C)

    a1, raw0, held, g1 = call(
        first_sent, [HBM] * 3, [A_ACT, A_RAW, A_WEIGHTS, A_HALF_GAINS],
        [RAW, GAIN, NATURAL, pltpu.SemaphoreType.DMA((6,)), pltpu.SemaphoreType.DMA((4,))],
    )(stay(features), stay(w1), stay(gain_first))
    a_far = to_next_pair(a1)
    w1, a0, a1 = call(
        rest_sent, [VM] * 4 + [HBM] * 3, [A_WEIGHTS, A_ACT, A_ACT],
        [
            GAIN, RAW, RAW, NATURAL, pltpu.SemaphoreType.DMA((2,)),
            pltpu.SemaphoreType.DMA((4,)), pltpu.SemaphoreType.DMA((4,)),
        ],
        aliases={3: 0},
    )(a1, raw0, g1, held, stay(features), stay(w1), stay(gain_first))
    a_earlier = shifted(a0)
    a_near = within_pair(a1)
    p1, wt1, wt2, m, g2, x0 = call(
        own_frames, [VM] * 3 + [HBM] * 3, [A_SUM, A_TURNED, A_TURNED, A_MASKS, A_GAINS, A_SLABS],
        [
            GAIN, pltpu.SMEM(video_frames.shape, jnp.int32), SLABS,
            pltpu.VMEM((TAPS * DEPTH, C), BF16), pltpu.SemaphoreType.DMA((3,)),
        ],
    )(a0, a1, w1, stay(w2), stay(gain_second), stay(video_frames))
    s1, x = call(halo_first, [VM] * 6, [A_ACT, A_SLABS])(a_far, a_near, p1, wt1, g2, m)
    s_before = shifted(s1)
    part = call(halo_middle, [VM] * 4, A_SUM)(x0, x, wt1, m)
    sent, x0 = call(halo_second, [VM] * 6, [A_ACT, A_SLABS], [SLABS])(a_earlier, part, wt1, wt2, g2, m)
    d_far = to_next_pair(sent)
    q0, q1, sent = call(near_second, [VM] * 3, [A_SUM, A_SUM, A_ACT], flops=10**10)(x0, wt2, m)
    d_near = within_pair(sent)
    q0, q1 = call(
        local_second, [VM] * 6, [A_SUM, A_SUM], [SLABS], aliases={4: 0, 5: 1}, flops=10**9
    )(x0, s1, wt2, m, q0, q1)
    whole = jax.ShapeDtypeStruct(features.shape, BF16)
    part, out = call(
        last_frame, [VM] * 6, [A_SUM, whole], [NATURAL, SLABS, FRAME, SEMS], [VM, ANY], flops=10**9,
    )(s_before, q0, q1, wt2, m, features)
    for kernel, d in ((from_far, d_far), (from_near, d_near)):
        out = call(
            kernel, [VM] * 4 + [ANY], whole, [NATURAL, FRAME, SEMS], ANY, {4: 0}
        )(d, part, m, features, out)
    return out


def solution(mesh):
    in_specs = (P(("group", "tm"), None, None, None), P("group"), P(), P(), P(), P())
    out_specs = P(("group", "tm"), None, None, None)
    return jax.shard_map(
        per_device, mesh=mesh, in_specs=in_specs, out_specs=out_specs, check_vma=False
    )
```

```python
import jax
import jax.numpy as jnp
from jax import lax
from jax.experimental import pallas as pl
from jax.experimental.pallas import tpu as pltpu
from jax.sharding import PartitionSpec as P

C = 192
ROWS = 8
COLS = 256
HALF = 128
TAPS = 3
SLAB = 3 * C
DEPTH = 9 * C
PIECE = 384
PARTS = 8
EPS = 1e-06
VMEM_LIMIT = 18 * 1024 * 1024
F32 = jnp.float32
BF16 = jnp.bfloat16


def shifted(value):
    return lax.ppermute(value, "tm", [(i, i + 1) for i in range(lax.axis_size("tm") - 1)])


def to_next_pair(value):
    return lax.ppermute(value, "tm", [(i, i + 1) for i in range(1, lax.axis_size("tm") - 1, 2)])


def within_pair(value):
    return lax.ppermute(value, "tm", [(i, i + 1) for i in range(0, lax.axis_size("tm"), 2)])


def tap_masks(frames_ref):
    first = 2 * lax.axis_index("tm")

    def step(v, carry):
        begin, start0, start1 = carry
        start0 = jnp.where(begin <= first, begin, start0)
        start1 = jnp.where(begin <= first + 1, begin, start1)
        return begin + frames_ref[v], start0, start1

    zero = jnp.int32(0)
    _, start0, start1 = lax.fori_loop(0, frames_ref.shape[0], step, (zero, zero, zero))
    return tuple(
        jnp.where(test, 1.0, 0.0).astype(F32)
        for test in (
            first - 1 >= start0,
            first - 2 >= start0,
            first >= start1,
            first - 1 >= start1,
        )
    )


def mask(m_ref, i):
    return m_ref[i : i + 1, :]


def turn_pieces(w_ref, wt_ref, taps):
    def turn(k, lo, hi):
        base = k * DEPTH
        wt_ref[k * C : (k + 1) * C, lo:hi] = w_ref[base + lo : base + hi, :].T

    return [
        (lambda k=k, lo=lo: turn(k, lo, min(lo + PIECE, DEPTH)))
        for k in taps
        for lo in range(0, DEPTH, PIECE)
    ]


def put_row(x_ref, row, values):
    base = (row + 1) * SLAB
    cols = lax.broadcasted_iota(jnp.int32, (C, COLS), 1)
    left = jnp.where(cols == 0, 0.0, pltpu.roll(values, 1, 1))
    right = jnp.where(cols == COLS - 1, 0.0, pltpu.roll(values, COLS - 1, 1))
    x_ref[base : base + C, :] = left.astype(BF16)
    x_ref[base + C : base + 2 * C, :] = values.astype(BF16)
    x_ref[base + 2 * C : base + 3 * C, :] = right.astype(BF16)


def clear_edges(x_ref):
    zeros = jnp.zeros((SLAB, COLS), BF16)
    x_ref[0:SLAB, :] = zeros
    x_ref[(ROWS + 1) * SLAB : (ROWS + 2) * SLAB, :] = zeros


def put(x_ref, a_ref, row):
    if row < ROWS:
        put_row(x_ref, row, a_ref[row].astype(F32))


def put_either(x_ref, far_ref, near_ref, row):
    if row < ROWS:
        put_row(x_ref, row, far_ref[row].astype(F32) + near_ref[row].astype(F32))


def product(wt_ref, lo, hi, x_ref, row):
    return jnp.dot(
        wt_ref[lo * C : hi * C, :],
        x_ref[row * SLAB : row * SLAB + DEPTH, :],
        preferred_element_type=F32,
    )


def sends_far():
    return lax.rem(lax.axis_index("tm"), 2) == 1


def inverse_rms(raw_ref, h):
    cols = slice(h * HALF, (h + 1) * HALF)

    def squares(b, total):
        v = raw_ref[pl.ds(b * 16, 16), :, cols].astype(F32)
        return total + jnp.sum(v * v, axis=0)

    total = lax.fori_loop(0, C // 16, squares, jnp.zeros((ROWS, HALF), F32))
    return lax.rsqrt(total * (1.0 / C) + EPS)


def activate(raw_ref, h, c, inverse, gain, t_ref):
    u = raw_ref[c, :, h * HALF : (h + 1) * HALF].astype(F32) * inverse * gain
    t_ref[h, c * ROWS : (c + 1) * ROWS, :] = u * jax.nn.sigmoid(u)


def row_of(t_ref, h, row):
    return t_ref[h, pl.ds(row, C, stride=ROWS), :]


def to_rows(t_ref, h, a_ref):
    for row in range(ROWS):
        a_ref[row, :, h * HALF : (h + 1) * HALF] = row_of(t_ref, h, row).astype(BF16)


def frame_copies(f_ref, index, raw_ref, sems):
    return [
        [
            pltpu.make_async_copy(
                f_ref.at[index, pl.ds(q * C // 2, C // 2), :, pl.ds(h * HALF, HALF)],
                raw_ref.at[pl.ds(q * C // 2, C // 2), :, pl.ds(h * HALF, HALF)],
                sems.at[2 * h + q],
            )
            for q in range(2)
        ]
        for h in range(2)
    ]


def taps_copy(w_any, w_ref, lo, hi, sem):
    span = pl.ds(lo * DEPTH, (hi - lo) * DEPTH)
    return pltpu.make_async_copy(w_any.at[span], w_ref.at[span], sem)


def flat(copies):
    return copies[0] + copies[1]


def activate_frame(raw_ref, gain, t_ref, a_ref, before=None, extra=None):
    for h in range(2):
        if before:
            before(h)
        inverse = inverse_rms(raw_ref, h)
        for c in range(C):
            activate(raw_ref, h, c, inverse, gain(c), t_ref)
            if extra and h == 0:
                extra(c)
        to_rows(t_ref, h, a_ref)


def waits(copies):
    def wait(h):
        for copy in copies[h]:
            copy.wait()

    return wait


def first_sent(
    f_ref, w1_any, gain_any, a_ref, raw0_ref, w_ref, g1_ref, raw1_ref, gain_ref, t_ref, sems, sems0
):
    @pl.when(sends_far())
    def _():
        copies = frame_copies(f_ref, 1, raw1_ref, sems)
        gains = pltpu.make_async_copy(gain_any, gain_ref, sems.at[4])
        later = [taps_copy(w1_any, w_ref, 0, 1, sems.at[5])] + flat(frame_copies(f_ref, 0, raw0_ref, sems0))
        for copy in copies[0] + [gains] + copies[1] + later:
            copy.start()

        def before(h):
            waits(copies)(h)
            if h == 0:
                gains.wait()

        def spread(c):
            g1_ref[c : c + 1, :] = jnp.full((1, HALF), gain_ref[c], F32)

        activate_frame(raw1_ref, lambda c: gain_ref[c], t_ref, a_ref, before, spread)
        for copy in later:
            copy.wait()


def rest_sent(
    a_ref, raw0_ref, g1_ref, _, f_ref, w1_any, gain_any,
    w_ref, a0_ref, a1_ref, gain_ref, raw_ref, last_ref, t_ref, sems, sems0, sems1,
):
    far = sends_far()

    @pl.when(far)
    def _():
        others = taps_copy(w1_any, w_ref, 1, TAPS, sems.at[0])
        others.start()
        a1_ref[...] = a_ref[...]
        activate_frame(raw0_ref, lambda c: g1_ref[c : c + 1, :], t_ref, a0_ref)
        others.wait()

    @pl.when(jnp.logical_not(far))
    def _():
        gains = pltpu.make_async_copy(gain_any, gain_ref, sems.at[0])
        first = taps_copy(w1_any, w_ref, 0, TAPS, sems.at[1])
        last = frame_copies(f_ref, 1, last_ref, sems1)
        other = frame_copies(f_ref, 0, raw_ref, sems0)
        for copy in last[0] + [gains] + last[1] + flat(other) + [first]:
            copy.start()
        gains.wait()
        activate_frame(last_ref, lambda c: gain_ref[c], t_ref, a1_ref, waits(last))
        activate_frame(raw_ref, lambda c: gain_ref[c], t_ref, a0_ref, waits(other))
        first.wait()


def second_activation(values, g_ref):
    mean_square = jnp.sum(values * values, axis=0, keepdims=True) * (1.0 / C)
    u = values * lax.rsqrt(mean_square + EPS) * g_ref[...]
    return (u * jax.nn.sigmoid(u)).astype(BF16)


def put_transposed(t_ref, row, values):
    t_ref[0, pl.ds(row, C, stride=ROWS), :] = values[:, :HALF]
    t_ref[1, pl.ds(row, C, stride=ROWS), :] = values[:, HALF:]


def own_frames(
    a0_ref, a1_ref, w1_ref, w2_any, gain2_any, frames_any,
    p1_ref, wt1_ref, wt2_ref, m_ref, g2_ref, x0_ref,
    gain2_ref, frames_ref, x1_ref, w2_ref, sems,
):
    small = [
        pltpu.make_async_copy(frames_any, frames_ref, sems.at[0]),
        pltpu.make_async_copy(gain2_any, gain2_ref, sems.at[1]),
    ]
    load = pltpu.make_async_copy(w2_any, w2_ref, sems.at[2])
    for copy in small + [load]:
        copy.start()
    for step in turn_pieces(w1_ref, wt1_ref, (0,)):
        step()
    clear_edges(x1_ref)
    clear_edges(x0_ref)
    put(x1_ref, a1_ref, 0)
    put(x1_ref, a1_ref, 1)
    turn1 = turn_pieces(w1_ref, wt1_ref, (1, 2))
    share = C // ROWS
    for row in range(ROWS):
        d = product(wt1_ref, 0, 1, x1_ref, row)
        put(x1_ref, a1_ref, row + 2)
        put(x0_ref, a0_ref, row)
        if row == 2:
            for copy in small:
                copy.wait()
            masks = tap_masks(frames_ref)
            for i in range(8):
                m_ref[i : i + 1, :] = jnp.full((1, COLS), masks[i % 4], F32)
        for step in turn1[row * len(turn1) // ROWS : (row + 1) * len(turn1) // ROWS]:
            step()
        p1_ref[row] = d
    load.wait()
    turn2 = turn_pieces(w2_ref, wt2_ref, (0, 1, 2))
    for row in range(ROWS):
        d = product(wt1_ref, 1, 2, x0_ref, row)
        for c in range(row * share, (row + 1) * share):
            g2_ref[c : c + 1, :] = jnp.full((1, COLS), gain2_ref[c], F32)
        for step in turn2[row * len(turn2) // ROWS : (row + 1) * len(turn2) // ROWS]:
            step()
        p1_ref[row] += mask(m_ref, 2) * d


def halo_first(far_ref, near_ref, o1_ref, wt_ref, g_ref, m_ref, s_ref, x_ref):
    clear_edges(x_ref)
    put_either(x_ref, far_ref, near_ref, 0)
    put_either(x_ref, far_ref, near_ref, 1)
    for row in range(ROWS):
        d = product(wt_ref, 2, 3, x_ref, row)
        put_either(x_ref, far_ref, near_ref, row + 2)
        s_ref[row] = second_activation(o1_ref[row] + mask(m_ref, 3) * d, g_ref)


def halo_middle(x0_ref, x_ref, wt_ref, m_ref, p_ref):
    for row in range(ROWS):
        d = mask(m_ref, 0) * product(wt_ref, 1, 2, x_ref, row)
        p_ref[row] = d + product(wt_ref, 0, 1, x0_ref, row)


def next_product(wt_ref, x_ref, sent_ref):
    for row in range(ROWS):
        sent_ref[row] = product(wt_ref, 2, 3, x_ref, row).astype(BF16)


def halo_second(h_ref, p_ref, wt1_ref, wt2_ref, g_ref, m_ref, sent_ref, x0_ref, x_ref):
    clear_edges(x_ref)
    clear_edges(x0_ref)
    put(x_ref, h_ref, 0)
    put(x_ref, h_ref, 1)
    for row in range(ROWS):
        d = product(wt1_ref, 2, 3, x_ref, row)
        put(x_ref, h_ref, row + 2)
        act = second_activation(p_ref[row] + mask(m_ref, 1) * d, g_ref)
        put_row(x0_ref, row, act.astype(F32))

    @pl.when(sends_far())
    def _():
        next_product(wt2_ref, x0_ref, sent_ref)


def first_part(x0_ref, wt_ref, m_ref, o0_ref, o1_ref):
    for row in range(ROWS):
        d = product(wt_ref, 0, 2, x0_ref, row)
        o0_ref[row] = d[:C]
        o1_ref[row] = mask(m_ref, 2) * d[C:]


def near_second(x0_ref, wt_ref, m_ref, o0_ref, o1_ref, sent_ref):
    @pl.when(jnp.logical_not(sends_far()))
    def _():
        next_product(wt_ref, x0_ref, sent_ref)
        first_part(x0_ref, wt_ref, m_ref, o0_ref, o1_ref)


def local_second(x0_ref, s1_ref, wt_ref, m_ref, _, __, o0_ref, o1_ref, x1_ref):
    @pl.when(sends_far())
    def _():
        first_part(x0_ref, wt_ref, m_ref, o0_ref, o1_ref)

    clear_edges(x1_ref)
    for row in range(ROWS):
        put(x1_ref, s1_ref, row)
    for row in range(ROWS):
        o1_ref[row] += product(wt_ref, 0, 1, x1_ref, row)


def finish(t_ref, f_ref, index, c, buf_ref):
    v = jnp.concatenate([t_ref[h, c * ROWS : (c + 1) * ROWS, :] for h in range(2)], axis=1)
    buf_ref[c] = (f_ref[index, c].astype(F32) + v).astype(BF16)


def write_frame(t_ref, f_ref, index, buf_ref, out_ref, sems):
    step = C // PARTS
    copies = []
    for part in range(PARTS):
        for c in range(part * step, (part + 1) * step):
            finish(t_ref, f_ref, index, c, buf_ref)
        span = pl.ds(part * step, step)
        copies.append(pltpu.make_async_copy(buf_ref.at[span], out_ref.at[index, span], sems.at[part]))
        copies[-1].start()
    for copy in copies:
        copy.wait()


def last_frame(h_ref, o0_ref, o1_ref, wt_ref, m_ref, f_ref, p_ref, out_ref, t_ref, x_ref, buf_ref, sems):
    clear_edges(x_ref)
    put(x_ref, h_ref, 0)
    put(x_ref, h_ref, 1)
    for row in range(ROWS):
        d = product(wt_ref, 1, 3, x_ref, row)
        put(x_ref, h_ref, row + 2)
        p_ref[row] = o0_ref[row] + mask(m_ref, 0) * d[:C]
        put_transposed(t_ref, row, o1_ref[row] + mask(m_ref, 3) * d[C:])
    write_frame(t_ref, f_ref, 1, buf_ref, out_ref, sems)


def first_frame(d_ref, p_ref, m_ref, f_ref, out_ref, t_ref, buf_ref, sems):
    for row in range(ROWS):
        put_transposed(t_ref, row, p_ref[row] + mask(m_ref, 1) * d_ref[row].astype(F32))
    write_frame(t_ref, f_ref, 0, buf_ref, out_ref, sems)


def from_far(d_ref, p_ref, m_ref, f_ref, _, out_ref, *scratch):
    @pl.when(jnp.logical_not(sends_far()))
    def _():
        first_frame(d_ref, p_ref, m_ref, f_ref, out_ref, *scratch)


def from_near(d_ref, p_ref, m_ref, f_ref, _, out_ref, *scratch):
    @pl.when(sends_far())
    def _():
        first_frame(d_ref, p_ref, m_ref, f_ref, out_ref, *scratch)


VM = pl.BlockSpec(memory_space=pltpu.VMEM)
ANY = pl.BlockSpec(memory_space=pl.ANY)
HBM = pl.BlockSpec(memory_space=pltpu.HBM)
NATURAL = pltpu.VMEM((2, C * ROWS, HALF), F32)
RAW = pltpu.VMEM((C, ROWS, COLS), BF16)
SLABS = pltpu.VMEM(((ROWS + 2) * SLAB, COLS), BF16)
FRAME = pltpu.VMEM((C, ROWS, COLS), BF16)
GAIN = pltpu.SMEM((C,), F32)
SEMS = pltpu.SemaphoreType.DMA((PARTS,))
A_SUM = jax.ShapeDtypeStruct((ROWS, C, COLS), F32)
A_ACT = jax.ShapeDtypeStruct((ROWS, C, COLS), BF16)
A_WEIGHTS = jax.ShapeDtypeStruct((TAPS * DEPTH, C), BF16)
A_RAW = jax.ShapeDtypeStruct((C, ROWS, COLS), BF16)
A_SLABS = jax.ShapeDtypeStruct(((ROWS + 2) * SLAB, COLS), BF16)
A_NATURAL = jax.ShapeDtypeStruct((2, C * ROWS, HALF), F32)
A_TURNED = jax.ShapeDtypeStruct((TAPS * C, DEPTH), BF16)
A_MASKS = jax.ShapeDtypeStruct((8, COLS), F32)
A_GAINS = jax.ShapeDtypeStruct((C, COLS), F32)
A_HALF_GAINS = jax.ShapeDtypeStruct((C, HALF), F32)


def stay(value):
    return pltpu.with_memory_space_constraint(value, pltpu.HBM)


def call(kernel, in_specs, out_shape, scratch=(), out_specs=None, aliases=None, flops=3 * 10**10):
    return pl.pallas_call(
        kernel,
        in_specs=in_specs,
        out_specs=out_specs or jax.tree.map(lambda _: VM, out_shape),
        out_shape=out_shape,
        scratch_shapes=scratch,
        input_output_aliases=aliases or {},
        compiler_params=pltpu.CompilerParams(vmem_limit_bytes=VMEM_LIMIT),
        cost_estimate=pl.CostEstimate(flops=flops, bytes_accessed=10**7, transcendentals=0),
        name=kernel.__name__,
    )


def per_device(features, video_frames, gain_first, conv_first, gain_second, conv_second):
    w1 = conv_first.reshape(TAPS * DEPTH, C)
    w2 = conv_second.reshape(TAPS * DEPTH, C)

    a1, raw0, held, g1 = call(
        first_sent, [HBM] * 3, [A_ACT, A_RAW, A_WEIGHTS, A_HALF_GAINS],
        [RAW, GAIN, NATURAL, pltpu.SemaphoreType.DMA((6,)), pltpu.SemaphoreType.DMA((4,))],
    )(stay(features), stay(w1), stay(gain_first))
    a_far = to_next_pair(a1)
    w1, a0, a1 = call(
        rest_sent, [VM] * 4 + [HBM] * 3, [A_WEIGHTS, A_ACT, A_ACT],
        [
            GAIN, RAW, RAW, NATURAL, pltpu.SemaphoreType.DMA((2,)),
            pltpu.SemaphoreType.DMA((4,)), pltpu.SemaphoreType.DMA((4,)),
        ],
        aliases={3: 0},
    )(a1, raw0, g1, held, stay(features), stay(w1), stay(gain_first))
    a_earlier = shifted(a0)
    a_near = within_pair(a1)
    p1, wt1, wt2, m, g2, x0 = call(
        own_frames, [VM] * 3 + [HBM] * 3, [A_SUM, A_TURNED, A_TURNED, A_MASKS, A_GAINS, A_SLABS],
        [
            GAIN, pltpu.SMEM(video_frames.shape, jnp.int32), SLABS,
            pltpu.VMEM((TAPS * DEPTH, C), BF16), pltpu.SemaphoreType.DMA((3,)),
        ],
    )(a0, a1, w1, stay(w2), stay(gain_second), stay(video_frames))
    s1, x = call(halo_first, [VM] * 6, [A_ACT, A_SLABS])(a_far, a_near, p1, wt1, g2, m)
    s_before = shifted(s1)
    part = call(halo_middle, [VM] * 4, A_SUM)(x0, x, wt1, m)
    sent, x0 = call(halo_second, [VM] * 6, [A_ACT, A_SLABS], [SLABS])(a_earlier, part, wt1, wt2, g2, m)
    d_far = to_next_pair(sent)
    q0, q1, sent = call(near_second, [VM] * 3, [A_SUM, A_SUM, A_ACT], flops=10**10)(x0, wt2, m)
    d_near = within_pair(sent)
    q0, q1 = call(
        local_second, [VM] * 6, [A_SUM, A_SUM], [SLABS], aliases={4: 0, 5: 1}, flops=10**9
    )(x0, s1, wt2, m, q0, q1)
    whole = jax.ShapeDtypeStruct(features.shape, BF16)
    part, out = call(
        last_frame, [VM] * 6, [A_SUM, whole], [NATURAL, SLABS, FRAME, SEMS], [VM, ANY], flops=10**9,
    )(s_before, q0, q1, wt2, m, features)
    for kernel, d in ((from_far, d_far), (from_near, d_near)):
        out = call(
            kernel, [VM] * 4 + [ANY], whole, [NATURAL, FRAME, SEMS], ANY, {4: 0}
        )(d, part, m, features, out)
    return out


def solution(mesh):
    in_specs = (P(("group", "tm"), None, None, None), P("group"), P(), P(), P(), P())
    out_specs = P(("group", "tm"), None, None, None)
    return jax.shard_map(
        per_device, mesh=mesh, in_specs=in_specs, out_specs=out_specs, check_vma=False
    )
```
